512 devices in a mesh: sub: 16 (over z), leaf: 32 (over y, x, core).
Axes of the slice: x: 4, y: 4, z: 16, core: 2. Of those that a mesh axis runs over, the one named last changes fastest.
Arguments:
- shift: float32 [1], replicated, may hold values from 0.5 to 2
- self_terms: float32 [524288], P(('leaf', 'sub')), may hold values from 1 to 2
- order: int32 [512, 1024], P(('leaf', 'sub')), may hold values from 0 to 1023, each once within a row
- split: int32 [512], P(('leaf', 'sub')), may hold values from 256 to 768
- coupling: bfloat16 [524288, 768], P(('leaf', 'sub')), as said below
- higher: bfloat16 [524288, 512], P(('leaf', 'sub'))
Outputs:
- applied_higher: bfloat16 [524288, 512], P(('leaf', 'sub'))
The draws below stay inside these ranges and needn't reach their ends.
Inputs may be any that keep to these rules, and one draw needn't show every extreme that they name: `coupling`: at every node of every level, the symmetric matrix made of diag and the blocks U V^T and V U^T of this and lower levels is positive definite.
All inputs are finite; a program needn't handle non-finite values.
Results may differ from the reference program's by a relative error of at most 0.001.
The reference program's roundings to bfloat16 on the way count: a program that leaves them out, or rounds other values in their place, can miss the bound.
Values sent between devices are 32-bit elements; how exact they have to be, the bound alone decides.
A program may use at most 64 MiB of HBM per device.

```python
import math
import jax
import jax.numpy as jnp
from jax import lax

RANK = 128
ROWS_DEV = 1024
HIGH = 4
WLEVELS = 6
BLOCKS = 512
ROWS = 524288
N_SUB = 16
N_LEAF = 32


def unit_levels(key):
    base = jax.random.fold_in(key, 101)
    shape = (ROWS, WLEVELS * RANK)
    return jax.random.normal(base, shape, jnp.float32)


def level_scales():
    child_rows = [ROWS_DEV // 2] + [ROWS_DEV * 2 ** (level - 1) for level in range(1, WLEVELS)]
    values = jnp.array([math.sqrt(0.14 / rows) for rows in child_rows], jnp.float32)
    return jnp.repeat(values, RANK)


def draw_coupling(key, part):
    return (unit_levels(key) * level_scales()[None, :]).astype(jnp.bfloat16)


def draw_higher(key, part):
    unit = unit_levels(key)
    noise_key = jax.random.fold_in(key, 211)
    shape = (ROWS, HIGH * RANK)
    noise = jax.random.normal(noise_key, shape, jnp.float32)
    mixing = jax.random.normal(jax.random.fold_in(key, 307), (WLEVELS, HIGH * RANK), jnp.float32)
    mixing = mixing * (0.9 / math.sqrt(WLEVELS))
    total = 0.3 * noise
    for level in range(WLEVELS):
        block = unit[:, level * RANK:(level + 1) * RANK]
        total = total + jnp.tile(block, (1, HIGH)) * mixing[level][None, :]
    return total.astype(jnp.bfloat16)


def place_ends(drawn, stream_key, smallest, top_value):
    longest = drawn.shape.index(max(drawn.shape))
    spots = []
    for shift in (0, 1):
        where = [jax.random.randint(jax.random.fold_in(stream_key, axis), (), 0, length) for axis, length in enumerate(drawn.shape)]
        where[longest] = (where[longest] + shift) % drawn.shape[longest]
        spots.append(tuple(where))
    return drawn.at[spots[0]].set(smallest).at[spots[1]].set(top_value)


def steps_of(key, shape, cuts, low, high):
    def one(position, blocks):
        draws = jax.random.uniform(jax.random.fold_in(jax.random.fold_in(key, 6), position), (blocks,), jnp.float32, low / len(cuts), high / len(cuts))
        return jnp.repeat(jnp.exp(draws), shape[position] // blocks).reshape((-1,) + (1,) * (len(shape) - position - 1))

    level = one(*cuts[0])
    for cut in cuts[1:]:
        level = level * one(*cut)
    return level


def setup_inputs(seed: int = 0) -> dict:
    splits = jax.random.split(jax.random.key(seed), 7)
    shift = jnp.clip(jnp.exp(jax.random.uniform(splits[0], (1,), jnp.float32, math.log(0.5), math.log(2.0))), 0.5, 2.0)
    self_terms = jnp.clip(1.0 + 1.0 * jax.random.uniform(splits[1], (ROWS,), jnp.float32) ** steps_of(splits[1], (ROWS,), ((0, 512),), -0.2, 0.2), 1.0, 2.0)
    order = jax.vmap(lambda own: jax.random.permutation(own, ROWS_DEV))(jax.random.split(splits[2], BLOCKS)).reshape((BLOCKS, ROWS_DEV)).astype(jnp.int32)
    split = place_ends(jax.random.randint(splits[3], (BLOCKS,), ROWS_DEV // 4, 3 * ROWS_DEV // 4 + 1), jax.random.fold_in(splits[3], 1), ROWS_DEV // 4, (3 * ROWS_DEV // 4 + 1) - 1).astype(jnp.int32)
    coupling = draw_coupling(jax.random.fold_in(splits[6], 71), 0)
    higher = draw_higher(jax.random.fold_in(splits[6], 71), 0)
    return dict(shift=shift, self_terms=self_terms, order=order, split=split, coupling=coupling, higher=higher)


def factor_solve(factor, target):
    lower_part = lax.linalg.triangular_solve(factor, target, left_side=True, lower=True)
    return lax.linalg.triangular_solve(factor, lower_part, left_side=True, lower=True, transpose_a=True)

def core_terms(left_sum, right_sum):
    width = left_sum.shape[0]
    first = left_sum[:, :width]
    projected = left_sum[:, width:]
    second = right_sum[:, :width]
    beyond = right_sum[:, width:]
    identity_block = jnp.eye(width, dtype=jnp.float32)
    first_factor = jnp.linalg.cholesky(first)
    first_inverse = factor_solve(first_factor, identity_block)
    schur_factor = jnp.linalg.cholesky(first_inverse - second)
    target = beyond - jnp.dot(second, projected, precision=lax.Precision.HIGHEST)
    back = factor_solve(schur_factor, target) - projected
    across = beyond + jnp.dot(second, back, precision=lax.Precision.HIGHEST)
    return (across, back)

def level_update(basis, columns, left, group_rows):
    total = columns.shape[0]
    nodes = total // group_rows
    width = basis.shape[1]
    inside = left.astype(jnp.float32)[:, None]
    basis_full = basis.astype(jnp.float32)
    cols_full = columns.astype(jnp.float32).reshape(nodes, group_rows, -1)
    left_basis = (basis_full * inside).reshape(nodes, group_rows, width)
    right_basis = (basis_full * (1.0 - inside)).reshape(nodes, group_rows, width)
    left_sum = jnp.einsum('ngr,ngw->nrw', left_basis, cols_full)
    right_sum = jnp.einsum('ngr,ngw->nrw', right_basis, cols_full)
    across, back = jax.vmap(core_terms)(left_sum, right_sum)
    left_coef = lax.optimization_barrier((-across).astype(jnp.bfloat16)).astype(jnp.float32)
    right_coef = lax.optimization_barrier(back.astype(jnp.bfloat16)).astype(jnp.float32)
    own = cols_full[:, :, :width]
    rest = cols_full[:, :, width:]
    inside_nodes = inside.reshape(nodes, group_rows, 1)
    update = rest + jnp.einsum('ngr,nrc->ngc', own * inside_nodes, left_coef)
    update = update + jnp.einsum('ngr,nrc->ngc', own * (1.0 - inside_nodes), right_coef)
    return lax.optimization_barrier(update.reshape(total, -1).astype(jnp.bfloat16))

def reference(shift, self_terms, order, split, coupling, higher):
    subtree_devices = 2 * N_SUB
    subtree_rows = subtree_devices * ROWS_DEV
    count = N_LEAF // 2

    def one_subtree(pieces):
        coupling_part, higher_part, terms_part, order_part, split_part = pieces
        diag = shift[0] + terms_part
        joined = jnp.concatenate([coupling_part, higher_part], axis=1).astype(jnp.float32)
        columns = lax.optimization_barrier((joined / diag[:, None]).astype(jnp.bfloat16))
        positions = jnp.arange(subtree_rows)
        for level in range(WLEVELS):
            basis = coupling_part[:, level * RANK:(level + 1) * RANK]
            if level == 0:
                left = (order_part < split_part[:, None]).reshape(-1)
                group_rows = ROWS_DEV
            else:
                group_rows = ROWS_DEV * 2 ** level
                left = positions // (group_rows // 2) % 2 == 0
            columns = level_update(basis, columns, left, group_rows)
        return columns
    result = lax.map(one_subtree, (coupling.reshape(count, subtree_rows, WLEVELS * RANK), higher.reshape(count, subtree_rows, HIGH * RANK), self_terms.reshape(count, subtree_rows), order.reshape(count, subtree_devices, ROWS_DEV), split.reshape(count, subtree_devices)))
    return result.reshape(ROWS, HIGH * RANK)
```

```python
import functools
import jax
import jax.numpy as jnp
from jax import lax
from jax.experimental import pallas as pl
from jax.experimental.pallas import tpu as pltpu
from jax.sharding import PartitionSpec as P

RANK = 128
CHUNK_ROWS = 64
PACE = 3
HIGHEST = lax.Precision.HIGHEST
VMEM = pltpu.VMEM


def dot32(a, b):
    return jnp.dot(a, b, precision=HIGHEST, preferred_element_type=jnp.float32)


def dot16(a, b):
    return jnp.dot(a, b, preferred_element_type=jnp.float32)


def identity():
    shape = (RANK, RANK)
    rows = lax.broadcasted_iota(jnp.int32, shape, 0)
    cols = lax.broadcasted_iota(jnp.int32, shape, 1)
    return jnp.where(rows == cols, 1.0, 0.0).astype(jnp.float32)


def symmetric(value):
    return 0.5 * (value + value.T)


def invert(other, mine, inv_ref, pow_ref):
    step = dot32(other, mine)
    inv_ref[...] = identity() + step
    power = dot32(step, step)
    pow_ref[...] = power

    def unfinished(carry):
        count, size = carry
        return (count < 48) & (size > 1e-16)

    def more(carry):
        count, _ = carry
        inverse = inv_ref[...]
        power = pow_ref[...]
        inv_ref[...] = inverse + dot32(inverse, power)
        power = dot32(power, power)
        pow_ref[...] = power
        return count + 1, jnp.sum(power * power)

    lax.while_loop(unfinished, more, (jnp.int32(0), jnp.sum(power * power)))


def column_blocks(count, body):
    pairs = count // 2

    @pl.loop(0, pairs)
    def _(pair):
        body(2 * pair, 2)

    if count % 2:
        body(count - 1, 1)


def lanes(start, width):
    first = start * RANK
    if not isinstance(first, int):
        first = pl.multiple_of(first, RANK)
    return pl.ds(first, width * RANK)


def side_by_side(ref, first, width):
    return jnp.concatenate([ref[first + i] for i in range(width)], axis=1)


def update_blocks(columns_ref, left_ref, coefs_of, next_ref, out_ref, partial_ref):
    count = out_ref.shape[1] // RANK

    def body(first, width):
        coef = coefs_of(first, width).astype(jnp.bfloat16)
        rest = columns_ref[:, lanes(first + 1, width)].astype(jnp.float32)
        fresh = (rest + dot16(left_ref[...], coef)).astype(jnp.bfloat16)
        out_ref[:, lanes(first, width)] = fresh
        if partial_ref is not None:
            sums = dot16(next_ref[...], fresh)
            for i in range(width):
                partial_ref[first + i] = sums[:, i * RANK : (i + 1) * RANK]

    column_blocks(count, body)


def start_kernel(
    shift_ref, split_ref, terms_ref, order_ref, coupling_ref, higher_ref,
    out_ref, partial_ref,
    columns_ref, own_ref, basis_t_ref, next_ref, sums_ref, mix_ref, inv_ref, pow_ref,
):
    rows = coupling_ref.shape[0]
    levels = coupling_ref.shape[1]
    shift = shift_ref[0]
    split = split_ref[0]
    for block in range(rows // RANK):
        here = pl.ds(block * RANK, RANK)
        diagonal = shift + terms_ref[pl.ds(block, 1), :]
        scale = jnp.broadcast_to(1.0 / diagonal, (RANK, RANK)).T
        mask = jnp.where(order_ref[pl.ds(block, 1), :] < split, 1.0, 0.0)
        inside_t = jnp.broadcast_to(mask, (RANK, RANK))
        inside = inside_t.T
        for first in range(0, levels, RANK):
            value = coupling_ref[here, pl.ds(first, RANK)].astype(jnp.float32)
            columns_ref[here, pl.ds(first, RANK)] = (value * scale).astype(jnp.bfloat16)
        for first in range(0, higher_ref.shape[1], RANK):
            value = higher_ref[here, pl.ds(first, RANK)].astype(jnp.float32)
            columns_ref[here, pl.ds(levels + first, RANK)] = (value * scale).astype(jnp.bfloat16)
        own = columns_ref[here, pl.ds(0, RANK)].astype(jnp.float32)
        own_ref[here, pl.ds(0, RANK)] = (own * inside).astype(jnp.bfloat16)
        own_ref[here, pl.ds(RANK, RANK)] = (own * (1.0 - inside)).astype(jnp.bfloat16)
        basis_t = coupling_ref[here, pl.ds(0, RANK)].astype(jnp.float32).T
        basis_t_ref[pl.ds(0, RANK), here] = (basis_t * inside_t).astype(jnp.bfloat16)
        basis_t_ref[pl.ds(RANK, RANK), here] = (basis_t * (1.0 - inside_t)).astype(jnp.bfloat16)
        later = coupling_ref[here, pl.ds(RANK, RANK)].astype(jnp.float32)
        next_ref[:, here] = later.T.astype(jnp.bfloat16)

    def project(first, width):
        sums_ref[:, lanes(first, width)] = dot16(
            basis_t_ref[...], columns_ref[:, lanes(first, width)]
        )

    column_blocks(columns_ref.shape[1] // RANK, project)
    first = symmetric(sums_ref[pl.ds(0, RANK), pl.ds(0, RANK)])
    second = symmetric(sums_ref[pl.ds(RANK, RANK), pl.ds(0, RANK)])
    invert(second, first, inv_ref, pow_ref)
    inverse = inv_ref[...]
    mix_ref[pl.ds(0, RANK), pl.ds(0, RANK)] = dot32(inverse, second)
    mix_ref[pl.ds(0, RANK), pl.ds(RANK, RANK)] = -inverse
    inverse = inverse.T
    mix_ref[pl.ds(RANK, RANK), pl.ds(0, RANK)] = -inverse
    mix_ref[pl.ds(RANK, RANK), pl.ds(RANK, RANK)] = dot32(inverse, first)

    def coefs_of(first, width):
        return dot32(mix_ref[...], sums_ref[:, lanes(first + 1, width)])

    update_blocks(columns_ref, own_ref, coefs_of, next_ref, out_ref, partial_ref)


def level_kernel(last, columns_ref, mine_ref, other_ref, *refs):
    if last:
        out_ref, own_ref, mix_ref, inv_ref, pow_ref = refs
        basis_ref = partial_ref = next_ref = None
    else:
        basis_ref, out_ref, partial_ref, own_ref, mix_ref, inv_ref, pow_ref, next_ref = refs
        for block in range(basis_ref.shape[0] // RANK):
            here = pl.ds(block * RANK, RANK)
            later = basis_ref[here, :].astype(jnp.float32)
            next_ref[:, here] = later.T.astype(jnp.bfloat16)
    own_ref[...] = columns_ref[:, pl.ds(0, RANK)]
    mine = symmetric(mine_ref[0])
    other = symmetric(other_ref[0])
    invert(other, mine, inv_ref, pow_ref)
    inverse = inv_ref[...]
    mix_ref[:, pl.ds(0, RANK)] = dot32(inverse, other)
    mix_ref[:, pl.ds(RANK, RANK)] = -inverse

    def coefs_of(first, width):
        sums = jnp.concatenate(
            [side_by_side(mine_ref, first + 1, width), side_by_side(other_ref, first + 1, width)],
            axis=0,
        )
        return dot32(mix_ref[...], sums)

    update_blocks(columns_ref, own_ref, coefs_of, next_ref, out_ref, partial_ref)


def start_call(shift, split, terms, order, coupling, higher):
    rows, levels = coupling.shape
    width = levels + higher.shape[1]
    rest = width - RANK
    whole = pl.BlockSpec(memory_space=VMEM)
    scalar = pl.BlockSpec(memory_space=pltpu.SMEM)
    return pl.pallas_call(
        start_kernel,
        name="start",
        out_shape=(
            jax.ShapeDtypeStruct((rows, rest), jnp.bfloat16),
            jax.ShapeDtypeStruct((rest // RANK, RANK, RANK), jnp.float32),
        ),
        in_specs=[scalar, scalar, whole, whole, whole, whole],
        out_specs=(whole, whole),
        scratch_shapes=[
            VMEM((rows, width), jnp.bfloat16),
            VMEM((rows, 2 * RANK), jnp.bfloat16),
            VMEM((2 * RANK, rows), jnp.bfloat16),
            VMEM((RANK, rows), jnp.bfloat16),
            VMEM((2 * RANK, width), jnp.float32),
            VMEM((2 * RANK, 2 * RANK), jnp.float32),
            VMEM((RANK, RANK), jnp.float32),
            VMEM((RANK, RANK), jnp.float32),
        ],
        compiler_params=pltpu.CompilerParams(vmem_limit_bytes=40 * 2**20),
    )(shift, split, terms.reshape(rows // RANK, RANK), order.reshape(rows // RANK, RANK), coupling, higher)


def level_call(level, columns, mine, other, coupling):
    rows, width = columns.shape
    rest = width - RANK
    last = coupling is None
    out_shape = [jax.ShapeDtypeStruct((rows, rest), jnp.bfloat16)]
    scratch = [
        VMEM((rows, RANK), jnp.bfloat16),
        VMEM((RANK, 2 * RANK), jnp.float32),
        VMEM((RANK, RANK), jnp.float32),
        VMEM((RANK, RANK), jnp.float32),
    ]

    def all_of(shape):
        return pl.BlockSpec(shape, lambda i: (0,) * len(shape))

    in_specs = [all_of(columns.shape), all_of(mine.shape), all_of(other.shape)]
    operands = [columns, mine, other]
    if not last:
        out_shape.append(jax.ShapeDtypeStruct((rest // RANK, RANK, RANK), jnp.float32))
        scratch.append(VMEM((RANK, rows), jnp.bfloat16))
        in_specs.append(pl.BlockSpec((rows, RANK), lambda i: (0, level + 1)))
        operands.append(coupling)
    return pl.pallas_call(
        functools.partial(level_kernel, last),
        name=f"level{level}",
        grid=(1,),
        out_shape=out_shape,
        in_specs=in_specs,
        out_specs=[all_of(shape.shape) for shape in out_shape],
        scratch_shapes=scratch,
        compiler_params=pltpu.CompilerParams(vmem_limit_bytes=40 * 2**20),
    )(*operands)


def share_kernel(
    span, kind, part_ref, mine_ref, other_ref,
    before, after, cross, up_buf, down_buf,
    before_sem, after_sem, cross_sem, up_sem, down_sem, pass_sem, swap_sem,
):
    chunks = part_ref.shape[0]
    place = lax.axis_index("sub")
    size = lax.axis_size("sub")
    leaf = lax.axis_index("leaf")
    above = {"sub": lax.rem(place + 1, size)}
    below = {"sub": lax.rem(place + size - 1, size)}
    partner = {"leaf": leaf + 1 - 2 * lax.rem(leaf, 2)}
    spot = lax.rem(place, span)
    first_child = lax.rem(place // span, 2) == 0
    has_below = spot > 0
    has_above = spot < span - 1
    if kind == "line":
        node_spot = lax.rem(place, 2 * span)
        link_below = node_spot > 0
        link_above = node_spot < 2 * span - 1
    elif kind == "core":
        link_below = has_below
        link_above = has_above
    barrier = pltpu.get_barrier_semaphore()
    if kind == "ring":
        pl.semaphore_signal(barrier, inc=1, device_id=below)
        pl.semaphore_signal(barrier, inc=1, device_id=above)
        pl.semaphore_wait(barrier, 2)
    else:

        @pl.when(link_below)
        def _():
            pl.semaphore_signal(barrier, inc=1, device_id=below)

        @pl.when(link_above)
        def _():
            pl.semaphore_signal(barrier, inc=1, device_id=above)

        greeted = link_below.astype(jnp.int32) + link_above.astype(jnp.int32)
        if kind == "core":
            pl.semaphore_signal(barrier, inc=1, device_id=partner)
            greeted = greeted + 1
        pl.semaphore_wait(barrier, greeted)

    def copy(src, dst, send, recv, c, to):
        return pltpu.make_async_remote_copy(
            src_ref=src.at[c], dst_ref=dst.at[c], send_sem=send.at[c], recv_sem=recv.at[c],
            device_id=to, device_id_type=pl.DeviceIdType.MESH,
        )

    def go_up(c):
        return copy(up_buf, before, up_sem, before_sem, c, above)

    def go_down(c):
        return copy(down_buf, after, down_sem, after_sem, c, below)

    def pass_up(c):
        return copy(cross, cross, pass_sem, cross_sem, c, above)

    def pass_down(c):
        return copy(cross, cross, pass_sem, cross_sem, c, below)

    def swap(c, to):
        return copy(mine_ref, cross, swap_sem, cross_sem, c, to)

    if kind == "line":
        distance = jnp.where(first_child, span - spot, spot + 1)
        forward_down = first_child & has_below
        forward_up = jnp.logical_not(first_child) & has_above
        swap_up = first_child & (spot == span - 1)
        swap_down = jnp.logical_not(first_child) & (spot == 0)
        cross_from = PACE * (span - 1 + distance)
    elif kind == "ring":
        half = span // 2
        upper = spot >= half
        distance = jnp.where(upper, span - spot, spot + 1)
        forward_down = upper & (spot > half)
        forward_up = jnp.logical_not(upper) & (spot < half - 1)
        swap_up = spot == span - 1
        swap_down = spot == 0
        cross_from = PACE * (span - 1 + distance)
    else:
        cross_from = PACE * jnp.maximum(spot, span - 1 - spot) + PACE

    up_from = PACE * spot
    down_from = PACE * (span - 1 - spot)
    sum_from = jnp.maximum(up_from, down_from)

    def within(c):
        return (c >= 0) & (c < chunks)

    if kind == "core":
        total_slots = chunks + PACE * (span - 1) + PACE
    elif kind == "ring":
        total_slots = chunks + PACE * (span - 1 + span // 2)
    else:
        total_slots = chunks + PACE * (2 * span - 1)

    @pl.loop(0, total_slots)
    def _(slot):
        if span > 1:
            c = slot - up_from

            @pl.when(within(c))
            def _():
                @pl.when(has_below)
                def _():
                    go_up(c).wait_recv()

                @pl.when(has_above & has_below)
                def _():
                    up_buf[c] = part_ref[c] + before[c]

                @pl.when(has_above & jnp.logical_not(has_below))
                def _():
                    up_buf[c] = part_ref[c]

                @pl.when(has_above)
                def _():
                    go_up(c).start()

            d = slot - down_from

            @pl.when(within(d))
            def _():
                @pl.when(has_above)
                def _():
                    go_down(d).wait_recv()

                @pl.when(has_above & has_below)
                def _():
                    down_buf[d] = part_ref[d] + after[d]

                @pl.when(has_below & jnp.logical_not(has_above))
                def _():
                    down_buf[d] = part_ref[d]

                @pl.when(has_below)
                def _():
                    go_down(d).start()

        e = slot - sum_from

        @pl.when(within(e))
        def _():
            if span == 1:
                mine_ref[e] = part_ref[e]
            else:

                @pl.when(has_above & has_below)
                def _():
                    mine_ref[e] = part_ref[e] + before[e] + after[e]

                @pl.when(has_below & jnp.logical_not(has_above))
                def _():
                    mine_ref[e] = part_ref[e] + before[e]

                @pl.when(has_above & jnp.logical_not(has_below))
                def _():
                    mine_ref[e] = part_ref[e] + after[e]

            if kind == "core":
                swap(e, partner).start()
            else:

                @pl.when(swap_up)
                def _():
                    swap(e, above).start()

                @pl.when(swap_down)
                def _():
                    swap(e, below).start()

        x = slot - cross_from

        @pl.when(within(x))
        def _():
            swap(x, partner).wait_recv()
            if kind != "core":

                @pl.when(forward_up)
                def _():
                    pass_up(x).start()

                @pl.when(forward_down)
                def _():
                    pass_down(x).start()

            other_ref[x] = cross[x]

    @pl.loop(0, chunks)
    def _(c):
        if span > 1:

            @pl.when(has_above)
            def _():
                go_up(c).wait_send()

            @pl.when(has_below)
            def _():
                go_down(c).wait_send()

        if kind == "core":
            swap(c, partner).wait_send()
        else:

            @pl.when(swap_up | swap_down)
            def _():
                swap(c, above).wait_send()

            @pl.when(forward_up | forward_down)
            def _():
                pass_up(c).wait_send()


def share_call(level, span, kind, partial):
    blocks = partial.shape[0]
    split = RANK // CHUNK_ROWS
    chunks = blocks * split
    shape = (chunks, CHUNK_ROWS, RANK)
    whole = pl.BlockSpec(memory_space=VMEM)
    buffer = VMEM(shape, jnp.float32)
    semaphores = pltpu.SemaphoreType.DMA((chunks,))
    mine, other = pl.pallas_call(
        functools.partial(share_kernel, span, kind),
        name=f"share{level}",
        out_shape=(jax.ShapeDtypeStruct(shape, jnp.float32),) * 2,
        in_specs=[whole],
        out_specs=(whole, whole),
        scratch_shapes=[buffer] * 5 + [semaphores] * 7,
        compiler_params=pltpu.CompilerParams(
            collective_id=level, has_side_effects=True, vmem_limit_bytes=24 * 2**20
        ),
    )(partial.reshape(shape))
    full = (blocks, RANK, RANK)
    return mine.reshape(full), other.reshape(full)


def per_device(shift, self_terms, order, split, coupling, higher):
    sub_bits = lax.axis_size("sub").bit_length() - 1
    columns, partial = start_call(shift, split, self_terms, order[0], coupling, higher)
    for level in range(1, sub_bits + 1):
        span = 2 ** (level - 1)
        kind = "ring" if level == sub_bits else "line"
        mine, other = share_call(level, span, kind, partial)
        columns, partial = level_call(level, columns, mine, other, coupling)
    mine, other = share_call(sub_bits + 1, lax.axis_size("sub"), "core", partial)
    (columns,) = level_call(sub_bits + 1, columns, mine, other, None)
    return columns


def solution(mesh):
    in_specs = (
        P(),
        P(("leaf", "sub")),
        P(("leaf", "sub"), None),
        P(("leaf", "sub")),
        P(("leaf", "sub"), None),
        P(("leaf", "sub"), None),
    )
    out_specs = P(("leaf", "sub"), None)
    return jax.shard_map(
        per_device, mesh=mesh, in_specs=in_specs, out_specs=out_specs, check_vma=False
    )
```

```python
import functools
import jax
import jax.numpy as jnp
from jax import lax
from jax.experimental import pallas as pl
from jax.experimental.pallas import tpu as pltpu
from jax.sharding import PartitionSpec as P

RANK = 128
PLANS = (("line", 384, 1), ("fold", 64, 8), ("fold", 128, 6), ("ring", 64, 12), ("core", 64, 9))
HIGHEST = lax.Precision.HIGHEST
VMEM = pltpu.VMEM


def dot32(a, b):
    return jnp.dot(a, b, precision=HIGHEST, preferred_element_type=jnp.float32)


def dot16(a, b):
    return jnp.dot(a, b, preferred_element_type=jnp.float32)


def halves(value):
    high = value.astype(jnp.bfloat16)
    return high, (value - high.astype(jnp.float32)).astype(jnp.bfloat16)


def store_mix(mix_ref, value):
    high, low = halves(value)
    depth = value.shape[1]
    mix_ref[:, pl.ds(0, depth)] = high
    mix_ref[:, pl.ds(depth, depth)] = high
    mix_ref[:, pl.ds(2 * depth, depth)] = low


def mixed(mix_ref, value):
    high, low = halves(value)
    return dot16(mix_ref[...], jnp.concatenate([high, low, high], axis=0))


def identity():
    shape = (RANK, RANK)
    rows = lax.broadcasted_iota(jnp.int32, shape, 0)
    cols = lax.broadcasted_iota(jnp.int32, shape, 1)
    return jnp.where(rows == cols, 1.0, 0.0).astype(jnp.float32)


def symmetric(value):
    return 0.5 * (value + value.T)


def invert(other, mine, inv_ref, pow_ref):
    step = dot32(other, mine)
    inv_ref[...] = identity() + step
    power = dot32(step, step)
    pow_ref[...] = power

    def unfinished(carry):
        count, size = carry
        return (count < 48) & (size > 1e-16)

    def more(carry):
        count, _ = carry
        inverse = inv_ref[...]
        power = pow_ref[...]
        inv_ref[...] = inverse + dot32(inverse, power)
        power = dot32(power, power)
        pow_ref[...] = power
        return count + 1, jnp.sum(power * power)

    lax.while_loop(unfinished, more, (jnp.int32(0), jnp.sum(power * power)))


def column_blocks(count, body):
    pairs = count // 2

    @pl.loop(0, pairs)
    def _(pair):
        body(2 * pair, 2)

    if count % 2:
        body(count - 1, 1)


def lanes(start, width):
    first = start * RANK
    if not isinstance(first, int):
        first = pl.multiple_of(first, RANK)
    return pl.ds(first, width * RANK)


def side_by_side(ref, first, width):
    return jnp.concatenate([ref[first + i] for i in range(width)], axis=1)


def update_blocks(columns_ref, left_of, coefs_of, next_ref, out_ref, partial_ref):
    count = out_ref.shape[1] // RANK

    def body(first, width):
        coef = coefs_of(first, width).astype(jnp.bfloat16)
        rest = columns_ref[:, lanes(first + 1, width)].astype(jnp.float32)
        fresh = (rest + dot16(left_of(), coef)).astype(jnp.bfloat16)
        out_ref[:, lanes(first, width)] = fresh
        if partial_ref is not None:
            sums = dot16(next_ref[...], fresh)
            for i in range(width):
                partial_ref[first + i] = sums[:, i * RANK : (i + 1) * RANK]

    column_blocks(count, body)


def start_kernel(
    shift_ref, split_ref, terms_ref, order_ref, coupling_ref, higher_ref,
    out_ref, partial_ref,
    columns_ref, own_ref, basis_t_ref, next_ref, sums_ref, mix_ref, inv_ref, pow_ref,
):
    rows, levels = coupling_ref.shape
    blocks = rows // RANK

    shift = shift_ref[0]
    split = split_ref[0]
    for block in range(blocks):
        here = pl.ds(block * RANK, RANK)
        diagonal = shift + terms_ref[pl.ds(block, 1), :]
        scale = jnp.broadcast_to(1.0 / diagonal, (RANK, RANK)).T
        mask = jnp.where(order_ref[pl.ds(block, 1), :] < split, 1.0, 0.0)
        inside_t = jnp.broadcast_to(mask, (RANK, RANK))
        inside = inside_t.T
        for first in range(0, levels, RANK):
            value = coupling_ref[here, pl.ds(first, RANK)].astype(jnp.float32)
            columns_ref[here, pl.ds(first, RANK)] = (value * scale).astype(jnp.bfloat16)
        own = columns_ref[here, pl.ds(0, RANK)].astype(jnp.float32)
        own_ref[here, pl.ds(0, RANK)] = (own * inside).astype(jnp.bfloat16)
        own_ref[here, pl.ds(RANK, RANK)] = (own * (1.0 - inside)).astype(jnp.bfloat16)
        basis_t = coupling_ref[here, pl.ds(0, RANK)].astype(jnp.float32).T
        basis_t_ref[pl.ds(0, RANK), here] = (basis_t * inside_t).astype(jnp.bfloat16)
        basis_t_ref[pl.ds(RANK, RANK), here] = (basis_t * (1.0 - inside_t)).astype(jnp.bfloat16)
        later = coupling_ref[here, pl.ds(RANK, RANK)].astype(jnp.float32)
        next_ref[:, here] = later.T.astype(jnp.bfloat16)
        for first in range(0, higher_ref.shape[1], RANK):
            value = higher_ref[here, pl.ds(first, RANK)].astype(jnp.float32)
            columns_ref[here, pl.ds(levels + first, RANK)] = (value * scale).astype(jnp.bfloat16)

    def project(first, width):
        sums_ref[:, lanes(first, width)] = dot16(
            basis_t_ref[...], columns_ref[:, lanes(first, width)]
        )

    column_blocks(columns_ref.shape[1] // RANK, project)
    first = symmetric(sums_ref[pl.ds(0, RANK), pl.ds(0, RANK)])
    second = symmetric(sums_ref[pl.ds(RANK, RANK), pl.ds(0, RANK)])
    invert(second, first, inv_ref, pow_ref)
    inverse = inv_ref[...]
    turned = inverse.T
    store_mix(
        mix_ref,
        jnp.concatenate(
            [
                jnp.concatenate([dot32(inverse, second), -inverse], axis=1),
                jnp.concatenate([-turned, dot32(turned, first)], axis=1),
            ],
            axis=0,
        ),
    )

    def coefs_of(first, width):
        return mixed(mix_ref, sums_ref[:, lanes(first + 1, width)])

    def left_of():
        return own_ref[...]

    update_blocks(columns_ref, left_of, coefs_of, next_ref, out_ref, partial_ref)


def level_kernel(level, last, folded, columns_ref, mine_ref, other_ref, *refs):
    if last:
        out_ref, mix_ref, inv_ref, pow_ref = refs
        partial_ref = next_ref = None
    else:
        coupling_ref, out_ref, partial_ref, mix_ref, inv_ref, pow_ref, next_ref = refs
        for block in range(coupling_ref.shape[0] // RANK):
            here = pl.ds(block * RANK, RANK)
            later = coupling_ref[here, pl.ds((level + 1) * RANK, RANK)].astype(jnp.float32)
            next_ref[:, here] = later.T.astype(jnp.bfloat16)
    mine = symmetric(mine_ref[0])
    other = symmetric(other_ref[0])
    invert(other, mine, inv_ref, pow_ref)
    inverse = inv_ref[...]
    beside = inverse if folded else -inverse
    store_mix(mix_ref, jnp.concatenate([dot32(inverse, other), beside], axis=1))

    def coefs_of(first, width):
        sums = jnp.concatenate(
            [side_by_side(mine_ref, first + 1, width), side_by_side(other_ref, first + 1, width)],
            axis=0,
        )
        return mixed(mix_ref, sums)

    def left_of():
        return columns_ref[:, pl.ds(0, RANK)]

    update_blocks(columns_ref, left_of, coefs_of, next_ref, out_ref, partial_ref)


def start_call(shift, split, terms, order, coupling, higher):
    rows, levels = coupling.shape
    width = levels + higher.shape[1]
    rest = width - RANK
    blocks = rows // RANK
    whole = pl.BlockSpec(memory_space=VMEM)
    scalar = pl.BlockSpec(memory_space=pltpu.SMEM)
    return pl.pallas_call(
        start_kernel,
        name="start",
        out_shape=(
            jax.ShapeDtypeStruct((rows, rest), jnp.bfloat16),
            jax.ShapeDtypeStruct((rest // RANK, RANK, RANK), jnp.float32),
        ),
        in_specs=[scalar, scalar, whole, whole, whole, whole],
        out_specs=(whole, whole),
        scratch_shapes=[
            VMEM((rows, width), jnp.bfloat16),
            VMEM((rows, 2 * RANK), jnp.bfloat16),
            VMEM((2 * RANK, rows), jnp.bfloat16),
            VMEM((RANK, rows), jnp.bfloat16),
            VMEM((2 * RANK, width), jnp.float32),
            VMEM((2 * RANK, 6 * RANK), jnp.bfloat16),
            VMEM((RANK, RANK), jnp.float32),
            VMEM((RANK, RANK), jnp.float32),
        ],
        compiler_params=pltpu.CompilerParams(vmem_limit_bytes=24 * 2**20),
    )(shift, split, terms.reshape(blocks, RANK), order.reshape(blocks, RANK), coupling, higher)


def level_call(level, folded, columns, mine, other, coupling):
    rows, width = columns.shape
    rest = width - RANK
    last = coupling is None
    out_shape = [jax.ShapeDtypeStruct((rows, rest), jnp.bfloat16)]
    scratch = [
        VMEM((RANK, 6 * RANK), jnp.bfloat16),
        VMEM((RANK, RANK), jnp.float32),
        VMEM((RANK, RANK), jnp.float32),
    ]
    operands = [columns, mine, other]
    if not last:
        out_shape.append(jax.ShapeDtypeStruct((rest // RANK, RANK, RANK), jnp.float32))
        scratch.append(VMEM((RANK, rows), jnp.bfloat16))
        operands.append(coupling)
    whole = pl.BlockSpec(memory_space=VMEM)
    return pl.pallas_call(
        functools.partial(level_kernel, level, last, folded),
        name=f"level{level}",
        out_shape=out_shape,
        in_specs=[whole] * len(operands),
        out_specs=[whole] * len(out_shape),
        scratch_shapes=scratch,
        compiler_params=pltpu.CompilerParams(vmem_limit_bytes=24 * 2**20),
    )(*operands)


def share_kernel(
    span, kind, pace, part_ref, mine_ref, other_ref,
    before, after, cross, up_buf, down_buf, half_ref, peer,
    before_sem, after_sem, cross_sem, up_sem, down_sem, pass_sem, swap_sem, trade_sem, peer_sem,
):
    chunks = part_ref.shape[0]
    place = lax.axis_index("sub")
    size = lax.axis_size("sub")
    leaf = lax.axis_index("leaf")
    above = {"sub": lax.rem(place + 1, size)}
    below = {"sub": lax.rem(place + size - 1, size)}
    partner = {"leaf": leaf + 1 - 2 * lax.rem(leaf, 2)}
    spot = lax.rem(place, span)
    first_child = lax.rem(place // span, 2) == 0
    has_below = spot > 0
    has_above = spot < span - 1
    barrier = pltpu.get_barrier_semaphore()
    if kind == "line":
        node_spot = lax.rem(place, 2 * span)
        link_below = node_spot > 0
        link_above = node_spot < 2 * span - 1

        @pl.when(link_above)
        def _():
            pl.semaphore_signal(barrier, inc=1, device_id=above)

        @pl.when(link_below)
        def _():
            pl.semaphore_signal(barrier, inc=1, device_id=below)

        pl.semaphore_wait(barrier, link_below.astype(jnp.int32) + link_above.astype(jnp.int32))
    else:
        pl.semaphore_signal(barrier, inc=1, device_id=below)
        pl.semaphore_signal(barrier, inc=1, device_id=above)
        if kind == "core":
            pl.semaphore_signal(barrier, inc=1, device_id=partner)
        pl.semaphore_wait(barrier, 3 if kind == "core" else 2)
    sum_ref = half_ref if kind == "core" else mine_ref

    def copy(src, dst, send, recv, c, to):
        return pltpu.make_async_remote_copy(
            src_ref=src.at[c], dst_ref=dst.at[c], send_sem=send.at[c], recv_sem=recv.at[c],
            device_id=to, device_id_type=pl.DeviceIdType.MESH,
        )

    def go_up(c):
        return copy(up_buf, before, up_sem, before_sem, c, above)

    def go_down(c):
        return copy(down_buf, after, down_sem, after_sem, c, below)

    def pass_on(c, to):
        return copy(cross, cross, pass_sem, cross_sem, c, to)

    def swap(c, to):
        return copy(sum_ref, cross, swap_sem, cross_sem, c, to)

    def trade(c):
        return copy(mine_ref, peer, trade_sem, peer_sem, c, partner)

    if kind == "line":
        reach = span
        distance = jnp.where(first_child, span - spot, spot + 1)
        forward_down = first_child & has_below
        forward_up = jnp.logical_not(first_child) & has_above
        swap_up = first_child & (spot == span - 1)
        swap_down = jnp.logical_not(first_child) & (spot == 0)
    else:
        reach = span // 2
        upper = spot >= reach
        distance = jnp.where(upper, span - spot, spot + 1)
        forward_down = upper & (spot > reach)
        forward_up = jnp.logical_not(upper) & (spot < reach - 1)
        swap_up = spot == span - 1
        swap_down = spot == 0
    up_from = pace * spot
    down_from = pace * (span - 1 - spot)
    sum_from = jnp.maximum(up_from, down_from)
    cross_from = pace * (span - 1 + distance)
    slots = chunks + pace * (span - 1 + reach)
    if kind == "core":
        slots += pace - 1

    def within(c):
        return (c >= 0) & (c < chunks)

    @pl.loop(0, slots)
    def _(slot):
        if span > 1:
            c = slot - up_from

            @pl.when(within(c))
            def _():
                @pl.when(has_below)
                def _():
                    go_up(c).wait_recv()

                @pl.when(has_above & has_below)
                def _():
                    up_buf[c] = part_ref[c] + before[c]

                @pl.when(has_above & jnp.logical_not(has_below))
                def _():
                    up_buf[c] = part_ref[c]

                @pl.when(has_above)
                def _():
                    go_up(c).start()

            d = slot - down_from

            @pl.when(within(d))
            def _():
                @pl.when(has_above)
                def _():
                    go_down(d).wait_recv()

                @pl.when(has_above & has_below)
                def _():
                    down_buf[d] = part_ref[d] + after[d]

                @pl.when(has_below & jnp.logical_not(has_above))
                def _():
                    down_buf[d] = part_ref[d]

                @pl.when(has_below)
                def _():
                    go_down(d).start()

        e = slot - sum_from

        @pl.when(within(e))
        def _():
            if span == 1:
                sum_ref[e] = part_ref[e]
            else:

                @pl.when(has_above & has_below)
                def _():
                    sum_ref[e] = part_ref[e] + before[e] + after[e]

                @pl.when(has_below & jnp.logical_not(has_above))
                def _():
                    sum_ref[e] = part_ref[e] + before[e]

                @pl.when(has_above & jnp.logical_not(has_below))
                def _():
                    sum_ref[e] = part_ref[e] + after[e]

            @pl.when(swap_up)
            def _():
                swap(e, above).start()

            @pl.when(swap_down)
            def _():
                swap(e, below).start()

        x = slot - cross_from

        @pl.when(within(x))
        def _():
            swap(x, above).wait_recv()
            if reach > 1:

                @pl.when(forward_up)
                def _():
                    pass_on(x, above).start()

                @pl.when(forward_down)
                def _():
                    pass_on(x, below).start()

            if kind == "core":
                mine_ref[x] = sum_ref[x] + cross[x]
                trade(x).start()
            else:
                other_ref[x] = cross[x]

        if kind == "core":
            y = slot - cross_from - (pace - 1)

            @pl.when(within(y))
            def _():
                trade(y).wait_recv()
                other_ref[y] = peer[y]

    @pl.loop(0, chunks)
    def _(c):
        if span > 1:

            @pl.when(has_above)
            def _():
                go_up(c).wait_send()

            @pl.when(has_below)
            def _():
                go_down(c).wait_send()

        @pl.when(swap_up | swap_down)
        def _():
            swap(c, above).wait_send()

        if reach > 1:

            @pl.when(forward_up | forward_down)
            def _():
                pass_on(c, above).wait_send()

        if kind == "core":
            trade(c).wait_send()


def fold_kernel(
    span, pace, part_ref, mine_ref, other_ref,
    before, after, cross, up_buf, down_buf, turned,
    before_sem, after_sem, cross_sem, up_sem, down_sem, pass_sem, swap_sem,
):
    chunks, height, _ = part_ref.shape
    head = RANK // height
    nodes = 2 * span
    place = lax.axis_index("sub")
    size = lax.axis_size("sub")
    above = {"sub": lax.rem(place + 1, size)}
    below = {"sub": lax.rem(place + size - 1, size)}
    spot = lax.rem(place, span)
    node_spot = lax.rem(place, nodes)
    first_child = node_spot < span
    second_child = jnp.logical_not(first_child)
    has_below = spot > 0
    has_above = spot < span - 1
    link_below = node_spot > 0
    link_above = node_spot < nodes - 1
    barrier = pltpu.get_barrier_semaphore()

    @pl.when(link_below)
    def _():
        pl.semaphore_signal(barrier, inc=1, device_id=below)

    @pl.when(link_above)
    def _():
        pl.semaphore_signal(barrier, inc=1, device_id=above)

    pl.semaphore_wait(barrier, link_below.astype(jnp.int32) + link_above.astype(jnp.int32))

    def copy(src, dst, send, recv, c, to):
        return pltpu.make_async_remote_copy(
            src_ref=src.at[c], dst_ref=dst.at[c], send_sem=send.at[c], recv_sem=recv.at[c],
            device_id=to, device_id_type=pl.DeviceIdType.MESH,
        )

    def go_up(c):
        return copy(up_buf, before, up_sem, before_sem, c, above)

    def go_down(c):
        return copy(down_buf, after, down_sem, after_sem, c, below)

    def pass_on(c, to):
        return copy(cross, cross, pass_sem, cross_sem, c, to)

    def swap(c, to):
        return copy(mine_ref, cross, swap_sem, cross_sem, c, to)

    forward_down = first_child & has_below
    forward_up = second_child & has_above
    swap_up = first_child & (spot == span - 1)
    swap_down = second_child & (spot == 0)
    distance = jnp.where(first_child, span - spot, spot + 1)
    cross_from = pace * (span - 1 + distance)
    up_from = pace * spot
    down_from = pace * (span - 1 - spot)
    sum_from = jnp.maximum(up_from, down_from)
    rise_from = pace * node_spot
    fall_from = pace * (nodes - 1 - node_spot)

    def in_head(c):
        return (c >= 0) & (c < head)

    def in_body(c):
        return (c >= head) & (c < chunks)

    @pl.loop(0, chunks + pace * (nodes - 1))
    def _(slot):
        c = slot - up_from

        @pl.when(in_head(c))
        def _():
            @pl.when(has_below)
            def _():
                go_up(c).wait_recv()

            @pl.when(has_above & has_below)
            def _():
                up_buf[c] = part_ref[c] + before[c]

            @pl.when(has_above & jnp.logical_not(has_below))
            def _():
                up_buf[c] = part_ref[c]

            @pl.when(has_above)
            def _():
                go_up(c).start()

        d = slot - down_from

        @pl.when(in_head(d))
        def _():
            @pl.when(has_above)
            def _():
                go_down(d).wait_recv()

            @pl.when(has_above & has_below)
            def _():
                down_buf[d] = part_ref[d] + after[d]

            @pl.when(has_below & jnp.logical_not(has_above))
            def _():
                down_buf[d] = part_ref[d]

            @pl.when(has_below)
            def _():
                go_down(d).start()

        e = slot - sum_from

        @pl.when(in_head(e))
        def _():
            @pl.when(has_above & has_below)
            def _():
                mine_ref[e] = part_ref[e] + before[e] + after[e]

            @pl.when(has_below & jnp.logical_not(has_above))
            def _():
                mine_ref[e] = part_ref[e] + before[e]

            @pl.when(has_above & jnp.logical_not(has_below))
            def _():
                mine_ref[e] = part_ref[e] + after[e]

            @pl.when(swap_up)
            def _():
                swap(e, above).start()

            @pl.when(swap_down)
            def _():
                swap(e, below).start()

        x = slot - cross_from

        @pl.when(in_head(x))
        def _():
            swap(x, above).wait_recv()

            @pl.when(forward_up)
            def _():
                pass_on(x, above).start()

            @pl.when(forward_down)
            def _():
                pass_on(x, below).start()

            other_ref[x] = cross[x]

        @pl.when((x == head - 1) & (forward_up | forward_down))
        def _():
            block = jnp.concatenate([cross[i] for i in range(head)], axis=0)
            for start in range(head, chunks, head):
                terms = jnp.concatenate([part_ref[start + i] for i in range(head)], axis=0)
                product = dot32(block, terms)
                for i in range(head):
                    turned[start + i] = product[i * height : (i + 1) * height, :]

        u = slot - rise_from

        @pl.when(in_body(u))
        def _():
            @pl.when(link_below)
            def _():
                go_up(u).wait_recv()

            @pl.when(first_child & jnp.logical_not(has_below))
            def _():
                value = part_ref[u]
                mine_ref[u] = value
                up_buf[u] = value

            @pl.when(first_child & has_below)
            def _():
                value = part_ref[u] + before[u]
                mine_ref[u] = value
                up_buf[u] = jnp.where(has_above, value, -value)

            @pl.when(second_child)
            def _():
                other_ref[u] = before[u]

            @pl.when(forward_up)
            def _():
                up_buf[u] = before[u] + turned[u]

            @pl.when(link_above)
            def _():
                go_up(u).start()

        v = slot - fall_from

        @pl.when(in_body(v))
        def _():
            @pl.when(link_above)
            def _():
                go_down(v).wait_recv()

            @pl.when(second_child & jnp.logical_not(has_above))
            def _():
                value = part_ref[v]
                mine_ref[v] = value
                down_buf[v] = value

            @pl.when(second_child & has_above)
            def _():
                value = part_ref[v] + after[v]
                mine_ref[v] = value
                down_buf[v] = jnp.where(has_below, value, -value)

            @pl.when(first_child)
            def _():
                other_ref[v] = after[v]

            @pl.when(forward_down)
            def _():
                down_buf[v] = after[v] + turned[v]

            @pl.when(link_below)
            def _():
                go_down(v).start()

    @pl.loop(0, head)
    def _(c):
        @pl.when(has_above)
        def _():
            go_up(c).wait_send()

        @pl.when(has_below)
        def _():
            go_down(c).wait_send()

        @pl.when(swap_up | swap_down)
        def _():
            swap(c, above).wait_send()

        @pl.when(forward_up | forward_down)
        def _():
            pass_on(c, above).wait_send()

    @pl.loop(head, chunks)
    def _(c):
        @pl.when(link_above)
        def _():
            go_up(c).wait_send()

        @pl.when(link_below)
        def _():
            go_down(c).wait_send()


def share_call(level, span, kind, height, pace, partial):
    blocks = partial.shape[0]
    chunks = blocks * RANK // height
    head = RANK // height
    shape = (chunks, height, RANK)
    whole = pl.BlockSpec(memory_space=VMEM)
    buffer = VMEM(shape, jnp.float32)
    semaphores = pltpu.SemaphoreType.DMA((chunks,))
    if kind == "fold":
        body = functools.partial(fold_kernel, span, pace)
        few = VMEM((head, height, RANK), jnp.float32)
        scratch = [buffer, buffer, few, buffer, buffer, buffer]
        some = pltpu.SemaphoreType.DMA((head,))
        scratch += [semaphores, semaphores, some, semaphores, semaphores, some, some]
    else:
        body = functools.partial(share_kernel, span, kind, pace)
        scratch = [buffer] * 7 + [semaphores] * 9
    mine, other = pl.pallas_call(
        body,
        name=f"share{level}",
        out_shape=(jax.ShapeDtypeStruct(shape, jnp.float32),) * 2,
        in_specs=[whole],
        out_specs=(whole, whole),
        scratch_shapes=scratch,
        compiler_params=pltpu.CompilerParams(
            collective_id=level, has_side_effects=True, vmem_limit_bytes=24 * 2**20
        ),
    )(partial.reshape(shape))
    full = (blocks, RANK, RANK)
    return mine.reshape(full), other.reshape(full)


def per_device(shift, self_terms, order, split, coupling, higher):
    size = lax.axis_size("sub")
    sub_bits = size.bit_length() - 1
    columns, partial = start_call(shift, split, self_terms, order[0], coupling, higher)
    for level in range(1, sub_bits + 1):
        span = 2 ** (level - 1)
        kind, height, pace = PLANS[level - 1]
        folded = kind == "fold"
        mine, other = share_call(level, span, kind, height, pace, partial)
        columns, partial = level_call(level, folded, columns, mine, other, coupling)
    kind, height, pace = PLANS[sub_bits]
    mine, other = share_call(sub_bits + 1, size // 2, kind, height, pace, partial)
    (columns,) = level_call(sub_bits + 1, False, columns, mine, other, None)
    return columns


def solution(mesh):
    in_specs = (
        P(),
        P(("leaf", "sub")),
        P(("leaf", "sub"), None),
        P(("leaf", "sub")),
        P(("leaf", "sub"), None),
        P(("leaf", "sub"), None),
    )
    out_specs = P(("leaf", "sub"), None)
    return jax.shard_map(
        per_device, mesh=mesh, in_specs=in_specs, out_specs=out_specs, check_vma=False
    )
```

```python
import functools
import jax
import jax.numpy as jnp
from jax import lax
from jax.experimental import pallas as pl
from jax.experimental.pallas import tpu as pltpu
from jax.sharding import PartitionSpec as P

RANK = 128
PLANS = (
    ("line", 384, 3, 3),
    ("fold", 128, 4, 2),
    ("fold", 64, 12, 2),
    ("ring", 64, 8, 2),
    ("core", 64, 9, 2),
)
HIGHEST = lax.Precision.HIGHEST
VMEM = pltpu.VMEM


def dot32(a, b):
    return jnp.dot(a, b, precision=HIGHEST, preferred_element_type=jnp.float32)


def dot16(a, b):
    return jnp.dot(a, b, preferred_element_type=jnp.float32)


def halves(value):
    high = value.astype(jnp.bfloat16)
    return high, (value - high.astype(jnp.float32)).astype(jnp.bfloat16)


def store_mix(mix_ref, value):
    high, low = halves(value)
    depth = value.shape[1]
    mix_ref[:, pl.ds(0, depth)] = high
    mix_ref[:, pl.ds(depth, depth)] = high
    mix_ref[:, pl.ds(2 * depth, depth)] = low


def mixed(mix_ref, value):
    high, low = halves(value)
    return dot16(mix_ref[...], jnp.concatenate([high, low, high], axis=0))


def identity():
    shape = (RANK, RANK)
    rows = lax.broadcasted_iota(jnp.int32, shape, 0)
    cols = lax.broadcasted_iota(jnp.int32, shape, 1)
    return jnp.where(rows == cols, 1.0, 0.0).astype(jnp.float32)


def symmetric(value):
    return 0.5 * (value + value.T)


def invert(other, mine, inv_ref, pow_ref):
    step = dot32(other, mine)
    inv_ref[...] = identity() + step
    power = dot32(step, step)
    pow_ref[...] = power

    def unfinished(carry):
        count, size = carry
        return (count < 48) & (size > 1e-16)

    def more(carry):
        count, _ = carry
        inverse = inv_ref[...]
        power = pow_ref[...]
        inv_ref[...] = inverse + dot32(inverse, power)
        power = dot32(power, power)
        pow_ref[...] = power
        return count + 1, jnp.sum(power * power)

    lax.while_loop(unfinished, more, (jnp.int32(0), jnp.sum(power * power)))


def column_blocks(count, body):
    pairs = count // 2

    @pl.loop(0, pairs)
    def _(pair):
        body(2 * pair, 2)

    if count % 2:
        body(count - 1, 1)


def lanes(start, width):
    first = start * RANK
    if not isinstance(first, int):
        first = pl.multiple_of(first, RANK)
    return pl.ds(first, width * RANK)


def side_by_side(ref, first, width):
    return jnp.concatenate([ref[first + i] for i in range(width)], axis=1)


def update(columns_ref, left_of, coefs_of, out_ref, first, width):
    coef = coefs_of(first, width).astype(jnp.bfloat16)
    rest = columns_ref[:, lanes(first + 1, width)].astype(jnp.float32)
    fresh = (rest + dot16(left_of(), coef)).astype(jnp.bfloat16)
    out_ref[:, lanes(first, width)] = fresh
    return fresh


def level_coefs(mine_ref, other_ref, mix_ref):
    def coefs_of(first, width):
        sums = jnp.concatenate(
            [side_by_side(mine_ref, first + 1, width), side_by_side(other_ref, first + 1, width)],
            axis=0,
        )
        return mixed(mix_ref, sums)

    return coefs_of


def solve(mine_ref, other_ref, folded, mix_ref, inv_ref, pow_ref):
    mine = symmetric(mine_ref[0])
    other = symmetric(other_ref[0])
    invert(other, mine, inv_ref, pow_ref)
    inverse = inv_ref[...]
    beside = inverse if folded else -inverse
    store_mix(mix_ref, jnp.concatenate([dot32(inverse, other), beside], axis=1))


def updates_in(share, level, height, wide, *refs):
    columns_ref, near_ref, far_ref, mix_ref, coupling_ref, out_ref, mine_ref, other_ref = refs[:8]
    next_ref, part_ref = refs[8:10]
    blocks = out_ref.shape[1] // RANK
    steps = wide * RANK // height
    full = blocks // wide
    if level == 1:

        def coefs_of(first, width):
            return mixed(mix_ref, far_ref[:, lanes(first + 1, width)])

        def left_of():
            return near_ref[...]

    else:
        coefs_of = level_coefs(near_ref, far_ref, mix_ref)

        def left_of():
            return columns_ref[:, pl.ds(0, RANK)]

    def prepare():
        for block in range(coupling_ref.shape[0] // RANK):
            here = pl.ds(block * RANK, RANK)
            later = coupling_ref[here, pl.ds(level * RANK, RANK)].astype(jnp.float32)
            next_ref[:, here] = later.T.astype(jnp.bfloat16)

    def make(step, width):
        first = step * wide
        fresh = update(columns_ref, left_of, coefs_of, out_ref, first, width)
        sums = dot16(next_ref[...], fresh)
        for i in range(width):
            block = sums[:, i * RANK : (i + 1) * RANK]
            if height > RANK:
                part_ref[step, pl.ds(i * RANK, RANK), :] = block
            else:
                pieces = RANK // height
                for piece in range(pieces):
                    rows = block[piece * height : (piece + 1) * height, :]
                    part_ref[(first + i) * pieces + piece] = rows

    def ready(slot):
        @pl.when((lax.rem(slot, steps) == 0) & (slot < full * steps))
        def _():
            make(slot // steps, wide)

        if blocks % wide:

            @pl.when(slot == full * steps)
            def _():
                make(full, blocks % wide)

    share(prepare, ready, part_ref, mine_ref, other_ref, *refs[10:])


def start_kernel(
    shift_ref, split_ref, terms_ref, order_ref, coupling_ref, higher_ref,
    columns_ref, own_ref, sums_ref, mix_ref,
    basis_t_ref, inv_ref, pow_ref,
):
    rows, levels = coupling_ref.shape
    blocks = rows // RANK

    shift = shift_ref[0]
    split = split_ref[0]
    for block in range(blocks):
        here = pl.ds(block * RANK, RANK)
        diagonal = shift + terms_ref[pl.ds(block, 1), :]
        scale = jnp.broadcast_to(1.0 / diagonal, (RANK, RANK)).T
        mask = jnp.where(order_ref[pl.ds(block, 1), :] < split, 1.0, 0.0)
        inside_t = jnp.broadcast_to(mask, (RANK, RANK))
        inside = inside_t.T
        for first in range(0, levels, RANK):
            value = coupling_ref[here, pl.ds(first, RANK)].astype(jnp.float32)
            columns_ref[here, pl.ds(first, RANK)] = (value * scale).astype(jnp.bfloat16)
        own = columns_ref[here, pl.ds(0, RANK)].astype(jnp.float32)
        own_ref[here, pl.ds(0, RANK)] = (own * inside).astype(jnp.bfloat16)
        own_ref[here, pl.ds(RANK, RANK)] = (own * (1.0 - inside)).astype(jnp.bfloat16)
        basis_t = coupling_ref[here, pl.ds(0, RANK)].astype(jnp.float32).T
        basis_t_ref[pl.ds(0, RANK), here] = (basis_t * inside_t).astype(jnp.bfloat16)
        basis_t_ref[pl.ds(RANK, RANK), here] = (basis_t * (1.0 - inside_t)).astype(jnp.bfloat16)
        for first in range(0, higher_ref.shape[1], RANK):
            value = higher_ref[here, pl.ds(first, RANK)].astype(jnp.float32)
            columns_ref[here, pl.ds(levels + first, RANK)] = (value * scale).astype(jnp.bfloat16)

    def project(first, width):
        sums_ref[:, lanes(first, width)] = dot16(
            basis_t_ref[...], columns_ref[:, lanes(first, width)]
        )

    column_blocks(columns_ref.shape[1] // RANK, project)
    first = symmetric(sums_ref[pl.ds(0, RANK), pl.ds(0, RANK)])
    second = symmetric(sums_ref[pl.ds(RANK, RANK), pl.ds(0, RANK)])
    invert(second, first, inv_ref, pow_ref)
    inverse = inv_ref[...]
    turned = inverse.T
    store_mix(
        mix_ref,
        jnp.concatenate(
            [
                jnp.concatenate([dot32(inverse, second), -inverse], axis=1),
                jnp.concatenate([-turned, dot32(turned, first)], axis=1),
            ],
            axis=0,
        ),
    )


def solve_kernel(folded, mine_ref, other_ref, mix_ref, inv_ref, pow_ref):
    solve(mine_ref, other_ref, folded, mix_ref, inv_ref, pow_ref)


def last_kernel(columns_ref, mine_ref, other_ref, out_ref, mix_ref, inv_ref, pow_ref):
    solve(mine_ref, other_ref, False, mix_ref, inv_ref, pow_ref)
    coefs_of = level_coefs(mine_ref, other_ref, mix_ref)

    def left_of():
        return columns_ref[:, pl.ds(0, RANK)]

    def body(first, width):
        update(columns_ref, left_of, coefs_of, out_ref, first, width)

    column_blocks(out_ref.shape[1] // RANK, body)


def start_call(shift, split, terms, order, coupling, higher):
    rows, levels = coupling.shape
    width = levels + higher.shape[1]
    blocks = rows // RANK
    whole = pl.BlockSpec(memory_space=VMEM)
    scalar = pl.BlockSpec(memory_space=pltpu.SMEM)
    return pl.pallas_call(
        start_kernel,
        name="start",
        out_shape=(
            jax.ShapeDtypeStruct((rows, width), jnp.bfloat16),
            jax.ShapeDtypeStruct((rows, 2 * RANK), jnp.bfloat16),
            jax.ShapeDtypeStruct((2 * RANK, width), jnp.float32),
            jax.ShapeDtypeStruct((2 * RANK, 6 * RANK), jnp.bfloat16),
        ),
        in_specs=[scalar, scalar, whole, whole, whole, whole],
        out_specs=(whole,) * 4,
        scratch_shapes=[
            VMEM((2 * RANK, rows), jnp.bfloat16),
            VMEM((RANK, RANK), jnp.float32),
            VMEM((RANK, RANK), jnp.float32),
        ],
        compiler_params=pltpu.CompilerParams(vmem_limit_bytes=24 * 2**20),
    )(shift, split, terms.reshape(blocks, RANK), order.reshape(blocks, RANK), coupling, higher)


def solve_call(level, folded, mine, other):
    square = VMEM((RANK, RANK), jnp.float32)
    whole = pl.BlockSpec(memory_space=VMEM)
    return pl.pallas_call(
        functools.partial(solve_kernel, folded),
        name=f"solve{level}",
        out_shape=jax.ShapeDtypeStruct((RANK, 6 * RANK), jnp.bfloat16),
        in_specs=[whole, whole],
        out_specs=whole,
        scratch_shapes=[square, square],
        compiler_params=pltpu.CompilerParams(vmem_limit_bytes=8 * 2**20),
    )(mine, other)


def last_call(columns, mine, other):
    rows, width = columns.shape
    square = VMEM((RANK, RANK), jnp.float32)
    whole = pl.BlockSpec(memory_space=VMEM)
    return pl.pallas_call(
        last_kernel,
        name="last",
        out_shape=jax.ShapeDtypeStruct((rows, width - RANK), jnp.bfloat16),
        in_specs=[whole] * 3,
        out_specs=whole,
        scratch_shapes=[VMEM((RANK, 6 * RANK), jnp.bfloat16), square, square],
        compiler_params=pltpu.CompilerParams(vmem_limit_bytes=24 * 2**20),
    )(columns, mine, other)


def share_kernel(
    span, kind, pace, prepare, ready, part_ref, mine_ref, other_ref,
    before, after, cross, up_buf, down_buf, half_ref, peer,
    before_sem, after_sem, cross_sem, up_sem, down_sem, pass_sem, swap_sem, trade_sem, peer_sem,
):
    chunks = part_ref.shape[0]
    place = lax.axis_index("sub")
    size = lax.axis_size("sub")
    leaf = lax.axis_index("leaf")
    above = {"sub": lax.rem(place + 1, size)}
    below = {"sub": lax.rem(place + size - 1, size)}
    partner = {"leaf": leaf + 1 - 2 * lax.rem(leaf, 2)}
    spot = lax.rem(place, span)
    first_child = lax.rem(place // span, 2) == 0
    has_below = spot > 0
    has_above = spot < span - 1
    barrier = pltpu.get_barrier_semaphore()
    if kind == "line":
        node_spot = lax.rem(place, 2 * span)
        link_below = node_spot > 0
        link_above = node_spot < 2 * span - 1

        @pl.when(link_above)
        def _():
            pl.semaphore_signal(barrier, inc=1, device_id=above)

        @pl.when(link_below)
        def _():
            pl.semaphore_signal(barrier, inc=1, device_id=below)

        prepare()
        pl.semaphore_wait(barrier, link_below.astype(jnp.int32) + link_above.astype(jnp.int32))
    else:
        pl.semaphore_signal(barrier, inc=1, device_id=below)
        pl.semaphore_signal(barrier, inc=1, device_id=above)
        if kind == "core":
            pl.semaphore_signal(barrier, inc=1, device_id=partner)
        prepare()
        pl.semaphore_wait(barrier, 3 if kind == "core" else 2)
    sum_ref = half_ref if kind == "core" else mine_ref

    def copy(src, dst, send, recv, c, to):
        return pltpu.make_async_remote_copy(
            src_ref=src.at[c], dst_ref=dst.at[c], send_sem=send.at[c], recv_sem=recv.at[c],
            device_id=to, device_id_type=pl.DeviceIdType.MESH,
        )

    def go_up(c):
        return copy(up_buf, before, up_sem, before_sem, c, above)

    def go_down(c):
        return copy(down_buf, after, down_sem, after_sem, c, below)

    def pass_on(c, to):
        return copy(cross, cross, pass_sem, cross_sem, c, to)

    def swap(c, to):
        return copy(sum_ref, cross, swap_sem, cross_sem, c, to)

    def trade(c):
        return copy(mine_ref, peer, trade_sem, peer_sem, c, partner)

    if kind == "line":
        reach = span
        distance = jnp.where(first_child, span - spot, spot + 1)
        forward_down = first_child & has_below
        forward_up = jnp.logical_not(first_child) & has_above
        swap_up = first_child & (spot == span - 1)
        swap_down = jnp.logical_not(first_child) & (spot == 0)
    else:
        reach = span // 2
        upper = spot >= reach
        distance = jnp.where(upper, span - spot, spot + 1)
        forward_down = upper & (spot > reach)
        forward_up = jnp.logical_not(upper) & (spot < reach - 1)
        swap_up = spot == span - 1
        swap_down = spot == 0
    up_from = pace * spot
    down_from = pace * (span - 1 - spot)
    sum_from = jnp.maximum(up_from, down_from)
    cross_from = pace * (span - 1 + distance)
    slots = chunks + pace * (span - 1 + reach)
    if kind == "core":
        slots += pace - 1

    def within(c):
        return (c >= 0) & (c < chunks)

    @pl.loop(0, slots)
    def _(slot):
        ready(slot)
        if span > 1:
            c = slot - up_from

            @pl.when(within(c))
            def _():
                @pl.when(has_below)
                def _():
                    go_up(c).wait_recv()

                @pl.when(has_above & has_below)
                def _():
                    up_buf[c] = part_ref[c] + before[c]

                @pl.when(has_above & jnp.logical_not(has_below))
                def _():
                    up_buf[c] = part_ref[c]

                @pl.when(has_above)
                def _():
                    go_up(c).start()

            d = slot - down_from

            @pl.when(within(d))
            def _():
                @pl.when(has_above)
                def _():
                    go_down(d).wait_recv()

                @pl.when(has_above & has_below)
                def _():
                    down_buf[d] = part_ref[d] + after[d]

                @pl.when(has_below & jnp.logical_not(has_above))
                def _():
                    down_buf[d] = part_ref[d]

                @pl.when(has_below)
                def _():
                    go_down(d).start()

        e = slot - sum_from

        @pl.when(within(e))
        def _():
            if span == 1:
                sum_ref[e] = part_ref[e]
            else:

                @pl.when(has_above & has_below)
                def _():
                    sum_ref[e] = part_ref[e] + before[e] + after[e]

                @pl.when(has_below & jnp.logical_not(has_above))
                def _():
                    sum_ref[e] = part_ref[e] + before[e]

                @pl.when(has_above & jnp.logical_not(has_below))
                def _():
                    sum_ref[e] = part_ref[e] + after[e]

            @pl.when(swap_up)
            def _():
                swap(e, above).start()

            @pl.when(swap_down)
            def _():
                swap(e, below).start()

        x = slot - cross_from

        @pl.when(within(x))
        def _():
            swap(x, above).wait_recv()
            if reach > 1:

                @pl.when(forward_up)
                def _():
                    pass_on(x, above).start()

                @pl.when(forward_down)
                def _():
                    pass_on(x, below).start()

            if kind == "core":
                mine_ref[x] = sum_ref[x] + cross[x]
                trade(x).start()
            else:
                other_ref[x] = cross[x]

        if kind == "core":
            y = slot - cross_from - (pace - 1)

            @pl.when(within(y))
            def _():
                trade(y).wait_recv()
                other_ref[y] = peer[y]

    @pl.loop(0, chunks)
    def _(c):
        if span > 1:

            @pl.when(has_above)
            def _():
                go_up(c).wait_send()

            @pl.when(has_below)
            def _():
                go_down(c).wait_send()

        @pl.when(swap_up | swap_down)
        def _():
            swap(c, above).wait_send()

        if reach > 1:

            @pl.when(forward_up | forward_down)
            def _():
                pass_on(c, above).wait_send()

        if kind == "core":
            trade(c).wait_send()


def fold_kernel(
    span, pace, prepare, ready, part_ref, mine_ref, other_ref,
    before, after, cross, up_buf, down_buf, turned,
    before_sem, after_sem, cross_sem, up_sem, down_sem, pass_sem, swap_sem,
):
    chunks, height, _ = part_ref.shape
    head = RANK // height
    nodes = 2 * span
    place = lax.axis_index("sub")
    size = lax.axis_size("sub")
    above = {"sub": lax.rem(place + 1, size)}
    below = {"sub": lax.rem(place + size - 1, size)}
    spot = lax.rem(place, span)
    node_spot = lax.rem(place, nodes)
    first_child = node_spot < span
    second_child = jnp.logical_not(first_child)
    has_below = spot > 0
    has_above = spot < span - 1
    link_below = node_spot > 0
    link_above = node_spot < nodes - 1
    barrier = pltpu.get_barrier_semaphore()

    @pl.when(link_below)
    def _():
        pl.semaphore_signal(barrier, inc=1, device_id=below)

    @pl.when(link_above)
    def _():
        pl.semaphore_signal(barrier, inc=1, device_id=above)

    prepare()
    pl.semaphore_wait(barrier, link_below.astype(jnp.int32) + link_above.astype(jnp.int32))

    def copy(src, dst, send, recv, c, to):
        return pltpu.make_async_remote_copy(
            src_ref=src.at[c], dst_ref=dst.at[c], send_sem=send.at[c], recv_sem=recv.at[c],
            device_id=to, device_id_type=pl.DeviceIdType.MESH,
        )

    def go_up(c):
        return copy(up_buf, before, up_sem, before_sem, c, above)

    def go_down(c):
        return copy(down_buf, after, down_sem, after_sem, c, below)

    def pass_on(c, to):
        return copy(cross, cross, pass_sem, cross_sem, c, to)

    def swap(c, to):
        return copy(mine_ref, cross, swap_sem, cross_sem, c, to)

    forward_down = first_child & has_below
    forward_up = second_child & has_above
    swap_up = first_child & (spot == span - 1)
    swap_down = second_child & (spot == 0)
    distance = jnp.where(first_child, span - spot, spot + 1)
    cross_from = pace * (span - 1 + distance)
    up_from = pace * spot
    down_from = pace * (span - 1 - spot)
    sum_from = jnp.maximum(up_from, down_from)
    rise_from = pace * node_spot
    fall_from = pace * (nodes - 1 - node_spot)

    def in_head(c):
        return (c >= 0) & (c < head)

    def in_body(c):
        return (c >= head) & (c < chunks)

    @pl.loop(0, chunks + pace * (nodes - 1))
    def _(slot):
        ready(slot)
        c = slot - up_from

        @pl.when(in_head(c))
        def _():
            @pl.when(has_below)
            def _():
                go_up(c).wait_recv()

            @pl.when(has_above & has_below)
            def _():
                up_buf[c] = part_ref[c] + before[c]

            @pl.when(has_above & jnp.logical_not(has_below))
            def _():
                up_buf[c] = part_ref[c]

            @pl.when(has_above)
            def _():
                go_up(c).start()

        d = slot - down_from

        @pl.when(in_head(d))
        def _():
            @pl.when(has_above)
            def _():
                go_down(d).wait_recv()

            @pl.when(has_above & has_below)
            def _():
                down_buf[d] = part_ref[d] + after[d]

            @pl.when(has_below & jnp.logical_not(has_above))
            def _():
                down_buf[d] = part_ref[d]

            @pl.when(has_below)
            def _():
                go_down(d).start()

        e = slot - sum_from

        @pl.when(in_head(e))
        def _():
            @pl.when(has_above & has_below)
            def _():
                mine_ref[e] = part_ref[e] + before[e] + after[e]

            @pl.when(has_below & jnp.logical_not(has_above))
            def _():
                mine_ref[e] = part_ref[e] + before[e]

            @pl.when(has_above & jnp.logical_not(has_below))
            def _():
                mine_ref[e] = part_ref[e] + after[e]

            @pl.when(swap_up)
            def _():
                swap(e, above).start()

            @pl.when(swap_down)
            def _():
                swap(e, below).start()

        x = slot - cross_from

        @pl.when(in_head(x))
        def _():
            swap(x, above).wait_recv()

            @pl.when(forward_up)
            def _():
                pass_on(x, above).start()

            @pl.when(forward_down)
            def _():
                pass_on(x, below).start()

            other_ref[x] = cross[x]

        @pl.when((x == head - 1) & (forward_up | forward_down))
        def _():
            block = jnp.concatenate([cross[i] for i in range(head)], axis=0)
            for start in range(head, chunks, head):
                terms = jnp.concatenate([part_ref[start + i] for i in range(head)], axis=0)
                product = dot32(block, terms)
                for i in range(head):
                    turned[start + i] = product[i * height : (i + 1) * height, :]

        u = slot - rise_from

        @pl.when(in_body(u))
        def _():
            @pl.when(link_below)
            def _():
                go_up(u).wait_recv()

            @pl.when(first_child & jnp.logical_not(has_below))
            def _():
                value = part_ref[u]
                mine_ref[u] = value
                up_buf[u] = value

            @pl.when(first_child & has_below)
            def _():
                value = part_ref[u] + before[u]
                mine_ref[u] = value
                up_buf[u] = jnp.where(has_above, value, -value)

            @pl.when(second_child)
            def _():
                other_ref[u] = before[u]

            @pl.when(forward_up)
            def _():
                up_buf[u] = before[u] + turned[u]

            @pl.when(link_above)
            def _():
                go_up(u).start()

        v = slot - fall_from

        @pl.when(in_body(v))
        def _():
            @pl.when(link_above)
            def _():
                go_down(v).wait_recv()

            @pl.when(second_child & jnp.logical_not(has_above))
            def _():
                value = part_ref[v]
                mine_ref[v] = value
                down_buf[v] = value

            @pl.when(second_child & has_above)
            def _():
                value = part_ref[v] + after[v]
                mine_ref[v] = value
                down_buf[v] = jnp.where(has_below, value, -value)

            @pl.when(first_child)
            def _():
                other_ref[v] = after[v]

            @pl.when(forward_down)
            def _():
                down_buf[v] = after[v] + turned[v]

            @pl.when(link_below)
            def _():
                go_down(v).start()

    @pl.loop(0, head)
    def _(c):
        @pl.when(has_above)
        def _():
            go_up(c).wait_send()

        @pl.when(has_below)
        def _():
            go_down(c).wait_send()

        @pl.when(swap_up | swap_down)
        def _():
            swap(c, above).wait_send()

        @pl.when(forward_up | forward_down)
        def _():
            pass_on(c, above).wait_send()

    @pl.loop(head, chunks)
    def _(c):
        @pl.when(link_above)
        def _():
            go_up(c).wait_send()

        @pl.when(link_below)
        def _():
            go_down(c).wait_send()


def share_call(level, span, columns, near, far, mix, coupling):
    kind, height, pace, wide = PLANS[level - 1]
    rows, width = columns.shape
    rest = width - RANK
    blocks = rest // RANK
    chunks = rest // height
    head = RANK // height
    shape = (chunks, height, RANK)
    whole = pl.BlockSpec(memory_space=VMEM)
    buffer = VMEM(shape, jnp.float32)
    semaphores = pltpu.SemaphoreType.DMA((chunks,))
    if kind == "fold":
        share = functools.partial(fold_kernel, span, pace)
        few = VMEM((head, height, RANK), jnp.float32)
        some = pltpu.SemaphoreType.DMA((head,))
        scratch = [buffer, buffer, few, buffer, buffer, buffer]
        scratch += [semaphores, semaphores, some, semaphores, semaphores, some, some]
    else:
        share = functools.partial(share_kernel, span, kind, pace)
        scratch = [buffer] * 7 + [semaphores] * 9
    columns, mine, other = pl.pallas_call(
        functools.partial(updates_in, share, level, height, wide),
        name=f"share{level}",
        out_shape=(
            jax.ShapeDtypeStruct((rows, rest), jnp.bfloat16),
            jax.ShapeDtypeStruct(shape, jnp.float32),
            jax.ShapeDtypeStruct(shape, jnp.float32),
        ),
        in_specs=[whole] * 5,
        out_specs=(whole,) * 3,
        scratch_shapes=[VMEM((RANK, rows), jnp.bfloat16), buffer] + scratch,
        compiler_params=pltpu.CompilerParams(
            collective_id=level, has_side_effects=True, vmem_limit_bytes=24 * 2**20
        ),
    )(columns, near, far, mix, coupling)
    squares = (blocks, RANK, RANK)
    return columns, mine.reshape(squares), other.reshape(squares)


def per_device(shift, self_terms, order, split, coupling, higher):
    size = lax.axis_size("sub")
    columns, near, far, mix = start_call(shift, split, self_terms, order[0], coupling, higher)
    for level in range(1, len(PLANS) + 1):
        kind = PLANS[level - 1][0]
        span = min(2 ** (level - 1), size // 2)
        columns, near, far = share_call(level, span, columns, near, far, mix, coupling)
        if level < len(PLANS):
            mix = solve_call(level, kind == "fold", near, far)
    return last_call(columns, near, far)


def solution(mesh):
    in_specs = (
        P(),
        P(("leaf", "sub")),
        P(("leaf", "sub"), None),
        P(("leaf", "sub")),
        P(("leaf", "sub"), None),
        P(("leaf", "sub"), None),
    )
    out_specs = P(("leaf", "sub"), None)
    return jax.shard_map(
        per_device, mesh=mesh, in_specs=in_specs, out_specs=out_specs, check_vma=False
    )
```

```python
import functools
import jax
import jax.numpy as jnp
from jax import lax
from jax.experimental import pallas as pl
from jax.experimental.pallas import tpu as pltpu
from jax.sharding import PartitionSpec as P

RANK = 128
PLANS = (
    ("line", 384, 3, 3),
    ("fold", 128, 4, 2),
    ("fold", 64, 12, 2),
    ("ring", 64, 8, 2),
    ("core", 64, 9, 2),
)
HIGHEST = lax.Precision.HIGHEST
VMEM = pltpu.VMEM


def dot32(a, b):
    return jnp.dot(a, b, precision=HIGHEST, preferred_element_type=jnp.float32)


def dot16(a, b):
    return jnp.dot(a, b, preferred_element_type=jnp.float32)


def halves(value):
    high = value.astype(jnp.bfloat16)
    return high, (value - high.astype(jnp.float32)).astype(jnp.bfloat16)


def store_mix(mix_ref, value):
    high, low = halves(value)
    depth = value.shape[1]
    mix_ref[:, pl.ds(0, depth)] = high
    mix_ref[:, pl.ds(depth, depth)] = high
    mix_ref[:, pl.ds(2 * depth, depth)] = low


def mixed(mix_ref, value):
    high, low = halves(value)
    return dot16(mix_ref[...], jnp.concatenate([high, low, high], axis=0))


def identity():
    shape = (RANK, RANK)
    rows = lax.broadcasted_iota(jnp.int32, shape, 0)
    cols = lax.broadcasted_iota(jnp.int32, shape, 1)
    return jnp.where(rows == cols, 1.0, 0.0).astype(jnp.float32)


def symmetric(value):
    return 0.5 * (value + value.T)


def invert(other, mine, inv_ref, pow_ref):
    step = dot32(other, mine)
    inv_ref[...] = identity() + step
    power = dot32(step, step)
    pow_ref[...] = power

    def unfinished(carry):
        count, size = carry
        return (count < 48) & (size > 1e-16)

    def more(carry):
        count, _ = carry
        inverse = inv_ref[...]
        power = pow_ref[...]
        inv_ref[...] = inverse + dot32(inverse, power)
        power = dot32(power, power)
        pow_ref[...] = power
        return count + 1, jnp.sum(power * power)

    lax.while_loop(unfinished, more, (jnp.int32(0), jnp.sum(power * power)))


def column_blocks(count, body):
    pairs = count // 2

    @pl.loop(0, pairs)
    def _(pair):
        body(2 * pair, 2)

    if count % 2:
        body(count - 1, 1)


def lanes(start, width):
    first = start * RANK
    if not isinstance(first, int):
        first = pl.multiple_of(first, RANK)
    return pl.ds(first, width * RANK)


def side_by_side(ref, first, width):
    return jnp.concatenate([ref[first + i] for i in range(width)], axis=1)


def update(columns_ref, left_of, coefs_of, out_ref, first, width):
    coef = coefs_of(first, width).astype(jnp.bfloat16)
    rest = columns_ref[:, lanes(first + 1, width)].astype(jnp.float32)
    fresh = (rest + dot16(left_of(), coef)).astype(jnp.bfloat16)
    out_ref[:, lanes(first, width)] = fresh
    return fresh


def level_coefs(mine_ref, other_ref, mix_ref):
    def coefs_of(first, width):
        sums = jnp.concatenate(
            [side_by_side(mine_ref, first + 1, width), side_by_side(other_ref, first + 1, width)],
            axis=0,
        )
        return mixed(mix_ref, sums)

    return coefs_of


def solve(mine_ref, other_ref, folded, mix_ref, inv_ref, pow_ref):
    mine = symmetric(mine_ref[0])
    other = symmetric(other_ref[0])
    invert(other, mine, inv_ref, pow_ref)
    inverse = inv_ref[...]
    beside = inverse if folded else -inverse
    store_mix(mix_ref, jnp.concatenate([dot32(inverse, other), beside], axis=1))


def updates_in(share, level, height, wide, *refs):
    columns_ref, near_ref, far_ref, mix_ref, coupling_ref, out_ref, mine_ref, other_ref = refs[:8]
    next_ref, part_ref = refs[8:10]
    blocks = out_ref.shape[1] // RANK
    steps = wide * RANK // height
    full = blocks // wide
    if level == 1:

        def coefs_of(first, width):
            return mixed(mix_ref, far_ref[:, lanes(first + 1, width)])

        def left_of():
            return near_ref[...]

    else:
        coefs_of = level_coefs(near_ref, far_ref, mix_ref)

        def left_of():
            return columns_ref[:, pl.ds(0, RANK)]

    def prepare():
        for block in range(coupling_ref.shape[0] // RANK):
            here = pl.ds(block * RANK, RANK)
            later = coupling_ref[here, pl.ds(level * RANK, RANK)].astype(jnp.float32)
            next_ref[:, here] = later.T.astype(jnp.bfloat16)

    def make(step, width):
        first = step * wide
        fresh = update(columns_ref, left_of, coefs_of, out_ref, first, width)
        sums = dot16(next_ref[...], fresh)
        for i in range(width):
            block = sums[:, i * RANK : (i + 1) * RANK]
            if height > RANK:
                part_ref[step, pl.ds(i * RANK, RANK), :] = block
            else:
                pieces = RANK // height
                for piece in range(pieces):
                    rows = block[piece * height : (piece + 1) * height, :]
                    part_ref[(first + i) * pieces + piece] = rows

    def ready(slot):
        @pl.when((lax.rem(slot, steps) == 0) & (slot < full * steps))
        def _():
            make(slot // steps, wide)

        if blocks % wide:

            @pl.when(slot == full * steps)
            def _():
                make(full, blocks % wide)

    share(prepare, ready, part_ref, mine_ref, other_ref, *refs[10:])


def start_kernel(
    rows_ref, coupling_ref, higher_ref,
    columns_ref, own_ref, sums_ref, mix_ref,
    basis_t_ref, inv_ref, pow_ref,
):
    rows, levels = coupling_ref.shape
    blocks = rows // RANK

    for block in range(blocks):
        here = pl.ds(block * RANK, RANK)
        scale = jnp.broadcast_to(rows_ref[pl.ds(block, 1), :], (RANK, RANK)).T
        inside_t = jnp.broadcast_to(rows_ref[pl.ds(blocks + block, 1), :], (RANK, RANK))
        inside = inside_t.T
        for first in range(0, levels, RANK):
            value = coupling_ref[here, pl.ds(first, RANK)].astype(jnp.float32)
            columns_ref[here, pl.ds(first, RANK)] = (value * scale).astype(jnp.bfloat16)
        own = columns_ref[here, pl.ds(0, RANK)].astype(jnp.float32)
        own_ref[here, pl.ds(0, RANK)] = (own * inside).astype(jnp.bfloat16)
        own_ref[here, pl.ds(RANK, RANK)] = (own * (1.0 - inside)).astype(jnp.bfloat16)
        basis_t = coupling_ref[here, pl.ds(0, RANK)].astype(jnp.float32).T
        basis_t_ref[pl.ds(0, RANK), here] = (basis_t * inside_t).astype(jnp.bfloat16)
        basis_t_ref[pl.ds(RANK, RANK), here] = (basis_t * (1.0 - inside_t)).astype(jnp.bfloat16)
        for first in range(0, higher_ref.shape[1], RANK):
            value = higher_ref[here, pl.ds(first, RANK)].astype(jnp.float32)
            columns_ref[here, pl.ds(levels + first, RANK)] = (value * scale).astype(jnp.bfloat16)

    def project(first, width):
        sums_ref[:, lanes(first, width)] = dot16(
            basis_t_ref[...], columns_ref[:, lanes(first, width)]
        )

    column_blocks(columns_ref.shape[1] // RANK, project)
    first = symmetric(sums_ref[pl.ds(0, RANK), pl.ds(0, RANK)])
    second = symmetric(sums_ref[pl.ds(RANK, RANK), pl.ds(0, RANK)])
    invert(second, first, inv_ref, pow_ref)
    inverse = inv_ref[...]
    turned = inverse.T
    store_mix(
        mix_ref,
        jnp.concatenate(
            [
                jnp.concatenate([dot32(inverse, second), -inverse], axis=1),
                jnp.concatenate([-turned, dot32(turned, first)], axis=1),
            ],
            axis=0,
        ),
    )


def solve_kernel(folded, mine_ref, other_ref, mix_ref, inv_ref, pow_ref):
    solve(mine_ref, other_ref, folded, mix_ref, inv_ref, pow_ref)


def last_kernel(columns_ref, mine_ref, other_ref, out_ref, mix_ref, inv_ref, pow_ref):
    solve(mine_ref, other_ref, False, mix_ref, inv_ref, pow_ref)
    coefs_of = level_coefs(mine_ref, other_ref, mix_ref)

    def left_of():
        return columns_ref[:, pl.ds(0, RANK)]

    def body(first, width):
        update(columns_ref, left_of, coefs_of, out_ref, first, width)

    column_blocks(out_ref.shape[1] // RANK, body)


def start_call(shift, split, terms, order, coupling, higher):
    rows, levels = coupling.shape
    width = levels + higher.shape[1]
    blocks = rows // RANK
    whole = pl.BlockSpec(memory_space=VMEM)
    scale = 1.0 / (shift[0] + terms)
    inside = (order < split[0]).astype(jnp.float32)
    per_row = jnp.concatenate([scale, inside]).reshape(2 * blocks, RANK)
    return pl.pallas_call(
        start_kernel,
        name="start",
        out_shape=(
            jax.ShapeDtypeStruct((rows, width), jnp.bfloat16),
            jax.ShapeDtypeStruct((rows, 2 * RANK), jnp.bfloat16),
            jax.ShapeDtypeStruct((2 * RANK, width), jnp.float32),
            jax.ShapeDtypeStruct((2 * RANK, 6 * RANK), jnp.bfloat16),
        ),
        in_specs=[whole] * 3,
        out_specs=(whole,) * 4,
        scratch_shapes=[
            VMEM((2 * RANK, rows), jnp.bfloat16),
            VMEM((RANK, RANK), jnp.float32),
            VMEM((RANK, RANK), jnp.float32),
        ],
        compiler_params=pltpu.CompilerParams(vmem_limit_bytes=24 * 2**20),
    )(per_row, coupling, higher)


def solve_call(level, folded, mine, other):
    square = VMEM((RANK, RANK), jnp.float32)
    whole = pl.BlockSpec(memory_space=VMEM)
    return pl.pallas_call(
        functools.partial(solve_kernel, folded),
        name=f"solve{level}",
        out_shape=jax.ShapeDtypeStruct((RANK, 6 * RANK), jnp.bfloat16),
        in_specs=[whole, whole],
        out_specs=whole,
        scratch_shapes=[square, square],
        compiler_params=pltpu.CompilerParams(vmem_limit_bytes=8 * 2**20),
    )(mine, other)


def last_call(columns, mine, other):
    rows, width = columns.shape
    square = VMEM((RANK, RANK), jnp.float32)
    whole = pl.BlockSpec(memory_space=VMEM)
    return pl.pallas_call(
        last_kernel,
        name="last",
        out_shape=jax.ShapeDtypeStruct((rows, width - RANK), jnp.bfloat16),
        in_specs=[whole] * 3,
        out_specs=whole,
        scratch_shapes=[VMEM((RANK, 6 * RANK), jnp.bfloat16), square, square],
        compiler_params=pltpu.CompilerParams(vmem_limit_bytes=24 * 2**20),
    )(columns, mine, other)


def share_kernel(
    span, kind, pace, prepare, ready, part_ref, mine_ref, other_ref,
    before, after, cross, up_buf, down_buf, half_ref, peer,
    before_sem, after_sem, cross_sem, up_sem, down_sem, pass_sem, swap_sem, trade_sem, peer_sem,
    skip_sem,
):
    chunks = part_ref.shape[0]
    place = lax.axis_index("sub")
    size = lax.axis_size("sub")
    leaf = lax.axis_index("leaf")
    above = {"sub": lax.rem(place + 1, size)}
    below = {"sub": lax.rem(place + size - 1, size)}
    partner = {"leaf": leaf + 1 - 2 * lax.rem(leaf, 2)}
    skip = 2 if kind == "core" else 1
    far_above = {"sub": lax.rem(place + skip, size)}
    far_below = {"sub": lax.rem(place + size - skip, size)}
    spot = lax.rem(place, span)
    first_child = lax.rem(place // span, 2) == 0
    has_below = spot > 0
    has_above = spot < span - 1
    barrier = pltpu.get_barrier_semaphore()
    if kind == "line":
        node_spot = lax.rem(place, 2 * span)
        link_below = node_spot > 0
        link_above = node_spot < 2 * span - 1

        @pl.when(link_above)
        def _():
            pl.semaphore_signal(barrier, inc=1, device_id=above)

        @pl.when(link_below)
        def _():
            pl.semaphore_signal(barrier, inc=1, device_id=below)

        prepare()
        pl.semaphore_wait(barrier, link_below.astype(jnp.int32) + link_above.astype(jnp.int32))
    else:
        pl.semaphore_signal(barrier, inc=1, device_id=below)
        pl.semaphore_signal(barrier, inc=1, device_id=above)
        if kind == "core":
            pl.semaphore_signal(barrier, inc=1, device_id=partner)
            pl.semaphore_signal(barrier, inc=1, device_id=far_below)
            pl.semaphore_signal(barrier, inc=1, device_id=far_above)
        prepare()
        pl.semaphore_wait(barrier, 5 if kind == "core" else 2)
    sum_ref = half_ref if kind == "core" else mine_ref

    def copy(src, dst, send, recv, c, to):
        return pltpu.make_async_remote_copy(
            src_ref=src.at[c], dst_ref=dst.at[c], send_sem=send.at[c], recv_sem=recv.at[c],
            device_id=to, device_id_type=pl.DeviceIdType.MESH,
        )

    def go_up(c):
        return copy(up_buf, before, up_sem, before_sem, c, above)

    def go_down(c):
        return copy(down_buf, after, down_sem, after_sem, c, below)

    def pass_on(c, to):
        return copy(cross, cross, pass_sem, cross_sem, c, to)

    def swap(c, to):
        return copy(sum_ref, cross, swap_sem, cross_sem, c, to)

    def swap_far(c, to):
        return copy(sum_ref, cross, skip_sem, cross_sem, c, to)

    def trade(c):
        return copy(mine_ref, peer, trade_sem, peer_sem, c, partner)

    if kind == "line":
        reach = span
        distance = jnp.where(first_child, span - spot, spot + 1)
        forward_down = first_child & has_below
        forward_up = jnp.logical_not(first_child) & has_above
        swap_up = first_child & (spot == span - 1)
        swap_down = jnp.logical_not(first_child) & (spot == 0)
    else:
        reach = span // 2
        upper = spot >= reach
        distance = jnp.where(upper, span - spot, spot + 1)
        forward_down = upper & (spot > reach + skip - 1)
        forward_up = jnp.logical_not(upper) & (spot < reach - skip)
        swap_up = spot == span - 1
        swap_down = spot == 0
    up_from = pace * spot
    down_from = pace * (span - 1 - spot)
    sum_from = jnp.maximum(up_from, down_from)
    cross_from = pace * (span - 1 + (distance + skip - 1) // skip)
    slots = chunks + pace * (span - 1 + reach // skip)
    if kind == "core":
        slots += pace - 1

    def within(c):
        return (c >= 0) & (c < chunks)

    @pl.loop(0, slots)
    def _(slot):
        ready(slot)
        if span > 1:
            c = slot - up_from

            @pl.when(within(c))
            def _():
                @pl.when(has_below)
                def _():
                    go_up(c).wait_recv()

                @pl.when(has_above & has_below)
                def _():
                    up_buf[c] = part_ref[c] + before[c]

                @pl.when(has_above & jnp.logical_not(has_below))
                def _():
                    up_buf[c] = part_ref[c]

                @pl.when(has_above)
                def _():
                    go_up(c).start()

            d = slot - down_from

            @pl.when(within(d))
            def _():
                @pl.when(has_above)
                def _():
                    go_down(d).wait_recv()

                @pl.when(has_above & has_below)
                def _():
                    down_buf[d] = part_ref[d] + after[d]

                @pl.when(has_below & jnp.logical_not(has_above))
                def _():
                    down_buf[d] = part_ref[d]

                @pl.when(has_below)
                def _():
                    go_down(d).start()

        e = slot - sum_from

        @pl.when(within(e))
        def _():
            if span == 1:
                sum_ref[e] = part_ref[e]
            else:

                @pl.when(has_above & has_below)
                def _():
                    sum_ref[e] = part_ref[e] + before[e] + after[e]

                @pl.when(has_below & jnp.logical_not(has_above))
                def _():
                    sum_ref[e] = part_ref[e] + before[e]

                @pl.when(has_above & jnp.logical_not(has_below))
                def _():
                    sum_ref[e] = part_ref[e] + after[e]

            @pl.when(swap_up)
            def _():
                swap(e, above).start()
                if skip > 1:
                    swap_far(e, far_above).start()

            @pl.when(swap_down)
            def _():
                swap(e, below).start()
                if skip > 1:
                    swap_far(e, far_below).start()

        x = slot - cross_from

        @pl.when(within(x))
        def _():
            swap(x, above).wait_recv()
            if reach > 1:

                @pl.when(forward_up)
                def _():
                    pass_on(x, far_above).start()

                @pl.when(forward_down)
                def _():
                    pass_on(x, far_below).start()

            if kind == "core":
                mine_ref[x] = sum_ref[x] + cross[x]
                trade(x).start()
            else:
                other_ref[x] = cross[x]

        if kind == "core":
            y = slot - cross_from - (pace - 1)

            @pl.when(within(y))
            def _():
                trade(y).wait_recv()
                other_ref[y] = peer[y]

    @pl.loop(0, chunks)
    def _(c):
        if span > 1:

            @pl.when(has_above)
            def _():
                go_up(c).wait_send()

            @pl.when(has_below)
            def _():
                go_down(c).wait_send()

        @pl.when(swap_up | swap_down)
        def _():
            swap(c, above).wait_send()
            if skip > 1:
                swap_far(c, far_above).wait_send()

        if reach > 1:

            @pl.when(forward_up | forward_down)
            def _():
                pass_on(c, far_above).wait_send()

        if kind == "core":
            trade(c).wait_send()


def fold_kernel(
    span, pace, prepare, ready, part_ref, mine_ref, other_ref,
    before, after, cross, up_buf, down_buf, turned,
    before_sem, after_sem, cross_sem, up_sem, down_sem, pass_sem, swap_sem,
):
    chunks, height, _ = part_ref.shape
    head = RANK // height
    nodes = 2 * span
    place = lax.axis_index("sub")
    size = lax.axis_size("sub")
    above = {"sub": lax.rem(place + 1, size)}
    below = {"sub": lax.rem(place + size - 1, size)}
    spot = lax.rem(place, span)
    node_spot = lax.rem(place, nodes)
    first_child = node_spot < span
    second_child = jnp.logical_not(first_child)
    has_below = spot > 0
    has_above = spot < span - 1
    link_below = node_spot > 0
    link_above = node_spot < nodes - 1
    barrier = pltpu.get_barrier_semaphore()

    @pl.when(link_below)
    def _():
        pl.semaphore_signal(barrier, inc=1, device_id=below)

    @pl.when(link_above)
    def _():
        pl.semaphore_signal(barrier, inc=1, device_id=above)

    prepare()
    pl.semaphore_wait(barrier, link_below.astype(jnp.int32) + link_above.astype(jnp.int32))

    def copy(src, dst, send, recv, c, to):
        return pltpu.make_async_remote_copy(
            src_ref=src.at[c], dst_ref=dst.at[c], send_sem=send.at[c], recv_sem=recv.at[c],
            device_id=to, device_id_type=pl.DeviceIdType.MESH,
        )

    def go_up(c):
        return copy(up_buf, before, up_sem, before_sem, c, above)

    def go_down(c):
        return copy(down_buf, after, down_sem, after_sem, c, below)

    def pass_on(c, to):
        return copy(cross, cross, pass_sem, cross_sem, c, to)

    def swap(c, to):
        return copy(mine_ref, cross, swap_sem, cross_sem, c, to)

    forward_down = first_child & has_below
    forward_up = second_child & has_above
    swap_up = first_child & (spot == span - 1)
    swap_down = second_child & (spot == 0)
    distance = jnp.where(first_child, span - spot, spot + 1)
    cross_from = pace * (span - 1 + distance)
    up_from = pace * spot
    down_from = pace * (span - 1 - spot)
    sum_from = jnp.maximum(up_from, down_from)
    rise_from = pace * node_spot
    fall_from = pace * (nodes - 1 - node_spot)

    def in_head(c):
        return (c >= 0) & (c < head)

    def in_body(c):
        return (c >= head) & (c < chunks)

    @pl.loop(0, chunks + pace * (nodes - 1))
    def _(slot):
        ready(slot)
        c = slot - up_from

        @pl.when(in_head(c))
        def _():
            @pl.when(has_below)
            def _():
                go_up(c).wait_recv()

            @pl.when(has_above & has_below)
            def _():
                up_buf[c] = part_ref[c] + before[c]

            @pl.when(has_above & jnp.logical_not(has_below))
            def _():
                up_buf[c] = part_ref[c]

            @pl.when(has_above)
            def _():
                go_up(c).start()

        d = slot - down_from

        @pl.when(in_head(d))
        def _():
            @pl.when(has_above)
            def _():
                go_down(d).wait_recv()

            @pl.when(has_above & has_below)
            def _():
                down_buf[d] = part_ref[d] + after[d]

            @pl.when(has_below & jnp.logical_not(has_above))
            def _():
                down_buf[d] = part_ref[d]

            @pl.when(has_below)
            def _():
                go_down(d).start()

        e = slot - sum_from

        @pl.when(in_head(e))
        def _():
            @pl.when(has_above & has_below)
            def _():
                mine_ref[e] = part_ref[e] + before[e] + after[e]

            @pl.when(has_below & jnp.logical_not(has_above))
            def _():
                mine_ref[e] = part_ref[e] + before[e]

            @pl.when(has_above & jnp.logical_not(has_below))
            def _():
                mine_ref[e] = part_ref[e] + after[e]

            @pl.when(swap_up)
            def _():
                swap(e, above).start()

            @pl.when(swap_down)
            def _():
                swap(e, below).start()

        x = slot - cross_from

        @pl.when(in_head(x))
        def _():
            swap(x, above).wait_recv()

            @pl.when(forward_up)
            def _():
                pass_on(x, above).start()

            @pl.when(forward_down)
            def _():
                pass_on(x, below).start()

            other_ref[x] = cross[x]

        @pl.when((x == head - 1) & (forward_up | forward_down))
        def _():
            high, low = halves(jnp.concatenate([cross[i] for i in range(head)], axis=0))
            block = jnp.concatenate([high, high, low], axis=1)
            for first in range(head, chunks, 2 * head):
                starts = range(first, min(first + 2 * head, chunks), head)
                terms = jnp.concatenate(
                    [
                        jnp.concatenate([part_ref[start + i] for i in range(head)], axis=0)
                        for start in starts
                    ],
                    axis=1,
                )
                high, low = halves(terms)
                product = dot16(block, jnp.concatenate([high, low, high], axis=0))
                for j, start in enumerate(starts):
                    for i in range(head):
                        piece = product[i * height : (i + 1) * height, j * RANK : (j + 1) * RANK]
                        turned[start + i] = piece

        u = slot - rise_from

        @pl.when(in_body(u))
        def _():
            @pl.when(link_below)
            def _():
                go_up(u).wait_recv()

            @pl.when(first_child & jnp.logical_not(has_below))
            def _():
                value = part_ref[u]
                mine_ref[u] = value
                up_buf[u] = value

            @pl.when(first_child & has_below)
            def _():
                value = part_ref[u] + before[u]
                mine_ref[u] = value
                up_buf[u] = jnp.where(has_above, value, -value)

            @pl.when(second_child)
            def _():
                other_ref[u] = before[u]

            @pl.when(forward_up)
            def _():
                up_buf[u] = before[u] + turned[u]

            @pl.when(link_above)
            def _():
                go_up(u).start()

        v = slot - fall_from

        @pl.when(in_body(v))
        def _():
            @pl.when(link_above)
            def _():
                go_down(v).wait_recv()

            @pl.when(second_child & jnp.logical_not(has_above))
            def _():
                value = part_ref[v]
                mine_ref[v] = value
                down_buf[v] = value

            @pl.when(second_child & has_above)
            def _():
                value = part_ref[v] + after[v]
                mine_ref[v] = value
                down_buf[v] = jnp.where(has_below, value, -value)

            @pl.when(first_child)
            def _():
                other_ref[v] = after[v]

            @pl.when(forward_down)
            def _():
                down_buf[v] = after[v] + turned[v]

            @pl.when(link_below)
            def _():
                go_down(v).start()

    @pl.loop(0, head)
    def _(c):
        @pl.when(has_above)
        def _():
            go_up(c).wait_send()

        @pl.when(has_below)
        def _():
            go_down(c).wait_send()

        @pl.when(swap_up | swap_down)
        def _():
            swap(c, above).wait_send()

        @pl.when(forward_up | forward_down)
        def _():
            pass_on(c, above).wait_send()

    @pl.loop(head, chunks)
    def _(c):
        @pl.when(link_above)
        def _():
            go_up(c).wait_send()

        @pl.when(link_below)
        def _():
            go_down(c).wait_send()


def share_call(level, span, columns, near, far, mix, coupling):
    kind, height, pace, wide = PLANS[level - 1]
    rows, width = columns.shape
    rest = width - RANK
    blocks = rest // RANK
    chunks = rest // height
    head = RANK // height
    shape = (chunks, height, RANK)
    whole = pl.BlockSpec(memory_space=VMEM)
    buffer = VMEM(shape, jnp.float32)
    semaphores = pltpu.SemaphoreType.DMA((chunks,))
    if kind == "fold":
        share = functools.partial(fold_kernel, span, pace)
        few = VMEM((head, height, RANK), jnp.float32)
        some = pltpu.SemaphoreType.DMA((head,))
        scratch = [buffer, buffer, few, buffer, buffer, buffer]
        scratch += [semaphores, semaphores, some, semaphores, semaphores, some, some]
    else:
        share = functools.partial(share_kernel, span, kind, pace)
        scratch = [buffer] * 7 + [semaphores] * 10
    columns, mine, other = pl.pallas_call(
        functools.partial(updates_in, share, level, height, wide),
        name=f"share{level}",
        out_shape=(
            jax.ShapeDtypeStruct((rows, rest), jnp.bfloat16),
            jax.ShapeDtypeStruct(shape, jnp.float32),
            jax.ShapeDtypeStruct(shape, jnp.float32),
        ),
        in_specs=[whole] * 5,
        out_specs=(whole,) * 3,
        scratch_shapes=[VMEM((RANK, rows), jnp.bfloat16), buffer] + scratch,
        compiler_params=pltpu.CompilerParams(
            collective_id=level, has_side_effects=True, vmem_limit_bytes=24 * 2**20
        ),
    )(columns, near, far, mix, coupling)
    squares = (blocks, RANK, RANK)
    return columns, mine.reshape(squares), other.reshape(squares)


def per_device(shift, self_terms, order, split, coupling, higher):
    size = lax.axis_size("sub")
    columns, near, far, mix = start_call(shift, split, self_terms, order[0], coupling, higher)
    for level in range(1, len(PLANS) + 1):
        kind = PLANS[level - 1][0]
        span = min(2 ** (level - 1), size // 2)
        columns, near, far = share_call(level, span, columns, near, far, mix, coupling)
        if level < len(PLANS):
            mix = solve_call(level, kind == "fold", near, far)
    return last_call(columns, near, far)


def solution(mesh):
    in_specs = (
        P(),
        P(("leaf", "sub")),
        P(("leaf", "sub"), None),
        P(("leaf", "sub")),
        P(("leaf", "sub"), None),
        P(("leaf", "sub"), None),
    )
    out_specs = P(("leaf", "sub"), None)
    return jax.shard_map(
        per_device, mesh=mesh, in_specs=in_specs, out_specs=out_specs, check_vma=False
    )
```
